32 devices in a mesh: groups: 2 (over x), row: 16 (over z, y, core).
Axes of the slice: x: 2, y: 2, z: 4, core: 2. Of those that a mesh axis runs over, the one named last changes fastest.
Arguments:
- matrix: float32 [32768, 1024], P(('groups', 'row')), parts along dimension 0, may hold values from -6 to 6
- leaf_vectors: float32 [4, 10240, 256], P('groups', 'row'), parts along dimension 0, may hold values from -0.25 to 0.25
- leaf_factors: float32 [4, 4096, 256], P('groups', 'row'), parts along dimension 0, as said below
- tree_vectors: float32 [4, 4096, 256], P('groups', 'row'), parts along dimension 0, may hold values from -0.375 to 0.375
- tree_factors: float32 [4, 4096, 256], P('groups', 'row'), parts along dimension 0, as said below
- leaf_blocks: int32 [4, 80], P('groups', 'row'), parts along dimension 0, may hold values from 0 to 7, as said below
- owner: int32 [4], P('groups'), parts along dimension 0, may hold values from 0 to 15
Outputs:
- updated: float32 [32768, 1024], P(('groups', 'row')), parts along dimension 0
The draws below stay inside these ranges and needn't reach their ends.
There are 2 independent parts, one for each index of `groups`. The reference program is written for one: setup_inputs(seed, part) draws one part's arguments, and reference() takes and returns one part's arrays. A program takes and returns all parts, laid end to end along the dimension named above; each array names one. Nothing has to cross between parts.
Inputs may be any that keep to these rules, and one draw needn't show every extreme that they name: `leaf_blocks`: in step s, the 5 entries of each grid block are distinct row-block numbers of that block: first the 2 blocks of the step's panel rows in order, last the block's final row block, the others between them. `leaf_factors`: each 256 x 256 factor is upper triangular. `tree_factors`: each 256 x 256 factor is upper triangular.
All inputs are finite; a program needn't handle non-finite values.
Results may differ from the reference program's by a relative error of at most 0.0001.
Values sent between devices are 32-bit elements; how exact they have to be, the bound alone decides.
A program may use at most 128 MiB of HBM per device.

```python
import math
import jax
import jax.numpy as jnp
from jax import lax

PW = 256
COLS = 1024
BLK = 128
NB = 5
STEPS = 2
ROWS_DEV = 1024
LEVELS = 4
ROWS = 16384
LEAF_ROWS = 10240
FACT_ROWS = 4096
BLOCK_LIST = 80
N_ROW = 16


def triangle(key):
    factor_count = FACT_ROWS // PW
    diag_key, off_key = jax.random.split(key)
    diagonal_part = jax.random.uniform(diag_key, (STEPS, factor_count, PW), jnp.float32, 0.5, 1.0)
    off_part = jax.random.normal(off_key, (STEPS, factor_count, PW, PW), jnp.float32) * (0.4 / math.sqrt(PW))
    row_index = lax.broadcasted_iota(jnp.int32, (PW, PW), 0)
    col_index = lax.broadcasted_iota(jnp.int32, (PW, PW), 1)
    triangular = jnp.where(col_index > row_index, off_part, 0.0)
    triangular = triangular + jnp.where(col_index == row_index, diagonal_part[..., :, None], 0.0)
    return triangular.reshape(STEPS, FACT_ROWS, PW).astype(jnp.float32)


def draw_leaf_factors(key, part):
    return triangle(jax.random.fold_in(key, 11))


def draw_tree_factors(key, part):
    return triangle(jax.random.fold_in(key, 23))


def draw_leaf_blocks(key, part):
    devices = BLOCK_LIST // NB
    block_count = ROWS_DEV // BLK
    per_panel = PW // BLK
    free_count = NB - per_panel - 1
    rows_out = []
    for step_index in range(STEPS):
        scores = jax.random.randint(jax.random.fold_in(key, 31 + step_index), (devices, block_count), 0, 1048576)
        col_index = lax.broadcasted_iota(jnp.int32, (devices, block_count), 1)
        scores = scores * block_count + col_index
        allowed = (col_index >= (step_index + 1) * per_panel) & (col_index <= block_count - 2)
        scores = jnp.where(allowed, scores, -1 - col_index)
        chosen = lax.top_k(scores, free_count)[1].astype(jnp.int32)
        panel_part = step_index * per_panel + lax.broadcasted_iota(jnp.int32, (devices, per_panel), 1)
        last_part = jnp.full((devices, 1), block_count - 1, jnp.int32)
        listed = jnp.concatenate([panel_part, chosen, last_part], axis=1)
        rows_out.append(listed.reshape(-1))
    return jnp.stack(rows_out).astype(jnp.int32)


def shard_levels(rng, extent, pieces, low, high):
    loudness = 1.0
    for dim, shards_of in pieces:
        heights = jax.random.uniform(jax.random.fold_in(jax.random.fold_in(rng, 6), dim), (shards_of,), jnp.float32, low / len(pieces), high / len(pieces))
        loudness = loudness * jnp.repeat(jnp.exp(heights), extent[dim] // shards_of).reshape((-1,) + (1,) * (len(extent) - 1 - dim))
    return loudness


def noise(own_key, dims, width, limit, cuts=(), kind=jnp.bfloat16):
    values = jax.random.normal(own_key, dims, jnp.float32) * width
    if len(cuts) > 0:
        values = shard_levels(own_key, dims, cuts, -0.22, 0.18) * values
    return jnp.clip(values, min=-limit, max=limit).astype(kind)


def setup_inputs(seed: int = 0, part: int = 0) -> dict:
    seeds = jax.random.split(jax.random.key(seed), 8)
    part_keys = jax.random.split(jax.random.fold_in(seeds[7], part), 8)
    matrix = noise(part_keys[0], (ROWS, COLS), 1.0, 6.0, ((0, 16),), jnp.float32)
    leaf_vectors = noise(part_keys[1], (STEPS, LEAF_ROWS, PW), (NB * BLK) ** -0.5, 0.25, ((1, 16),), jnp.float32)
    leaf_factors = draw_leaf_factors(jax.random.fold_in(jax.random.fold_in(seeds[7], part), 71), part)
    tree_vectors = noise(part_keys[3], (STEPS, FACT_ROWS, PW), PW ** -0.5, 0.375, ((1, 16),), jnp.float32)
    tree_factors = draw_tree_factors(jax.random.fold_in(jax.random.fold_in(seeds[7], part), 71), part)
    leaf_blocks = draw_leaf_blocks(jax.random.fold_in(jax.random.fold_in(seeds[7], part), 71), part)
    owner = jax.random.randint(part_keys[6], (STEPS,), 0, N_ROW).astype(jnp.int32)
    return {"matrix": matrix, "leaf_vectors": leaf_vectors, "leaf_factors": leaf_factors, "tree_vectors": tree_vectors, "tree_factors": tree_factors, "leaf_blocks": leaf_blocks, "owner": owner}


def product(spec_text, left_side, right_side):
    return jnp.einsum(spec_text, left_side, right_side, precision=lax.Precision.HIGHEST)


def tree_combine(top_rows, tree_y, tree_t, owner_now):
    relative_tops = jnp.roll(top_rows, -owner_now, axis=0)
    relative_y = jnp.roll(tree_y, -owner_now, axis=0)
    relative_t = jnp.roll(tree_t, -owner_now, axis=0)
    for tree_level in range(LEVELS):
        partner_gap = 2 ** tree_level
        pair_count = N_ROW // (2 * partner_gap)
        grouped = relative_tops.reshape(pair_count, 2, partner_gap, PW, COLS)
        upper_rows = grouped[:, 0, 0]
        lower_rows = grouped[:, 1, 0]
        vector_lower = relative_y.reshape(pair_count, 2, partner_gap, PW, PW)[:, 1, 0]
        factor_lower = relative_t.reshape(pair_count, 2, partner_gap, PW, PW)[:, 1, 0]
        projected = product("gkp,gkc->gpc", vector_lower, lower_rows)
        update = product("gkp,gkc->gpc", factor_lower, upper_rows + projected)
        grouped = grouped.at[:, 0, 0].set(upper_rows - update)
        grouped = grouped.at[:, 1, 0].set(lower_rows - product("gpk,gkc->gpc", vector_lower, update))
        relative_tops = grouped.reshape(N_ROW, PW, COLS)
    return jnp.roll(relative_tops, owner_now, axis=0)


def reference(matrix, leaf_vectors, leaf_factors, tree_vectors, tree_factors, leaf_blocks, owner):
    block_count = ROWS_DEV // BLK
    work_matrix = matrix.reshape(N_ROW, block_count, BLK, COLS)
    device_ids = jnp.arange(N_ROW).astype(jnp.int32)[:, None]
    for step_index in range(STEPS):
        listed = leaf_blocks[step_index].reshape(N_ROW, NB).astype(jnp.int32)
        gathered = work_matrix[device_ids, listed].reshape(N_ROW, NB * BLK, COLS)
        vectors = leaf_vectors[step_index].reshape(N_ROW, NB * BLK, PW)
        factors = leaf_factors[step_index].reshape(N_ROW, PW, PW)
        projected = product("nrp,nrc->npc", vectors, gathered)
        update = product("nkp,nkc->npc", factors, projected)
        renewed = gathered - product("nrp,npc->nrc", vectors, update)
        work_matrix = work_matrix.at[device_ids, listed].set(renewed.reshape(N_ROW, NB, BLK, COLS))
        by_device = work_matrix.reshape(N_ROW, ROWS_DEV, COLS)
        top_rows = by_device[:, step_index * PW:(step_index + 1) * PW]
        top_rows = tree_combine(top_rows, tree_vectors[step_index].reshape(N_ROW, PW, PW),
                                tree_factors[step_index].reshape(N_ROW, PW, PW), owner[step_index])
        by_device = by_device.at[:, step_index * PW:(step_index + 1) * PW].set(top_rows)
        work_matrix = by_device.reshape(N_ROW, block_count, BLK, COLS)
    return work_matrix.reshape(N_ROW * ROWS_DEV, COLS)
```

```python
import functools

import jax
import jax.numpy as jnp
import numpy as np
from jax import lax
from jax.experimental import pallas as pl
from jax.experimental.pallas import tpu as pltpu
from jax.sharding import PartitionSpec as P

BLK = 128
STEPS = 2
COLS_PER_LEAF = 256

PLANNED_ROWS = 16
HALF_ODD = (1, 1, 1, 1)
HALF_EVEN = (2, 2, 4)
TOP_ODD = (1, 1)
TOP_EVEN = (0, 0, 0, 0, 0)
SLOTS = 4

NN = (((1,), (0,)), ((), ()))
TN = (((0,), (0,)), ((), ()))
NT = (((1,), (1,)), ((), ()))


def split(value):
    high = value.astype(jnp.bfloat16)
    low = (value - high.astype(jnp.float32)).astype(jnp.bfloat16)
    return high, low


def product3(left, right, dims):
    def one(a, b):
        return lax.dot_general(a, b, dims, preferred_element_type=jnp.float32)

    return one(left[0], right[0]) + (one(left[0], right[1]) + one(left[1], right[0]))


def corner_masks(half):
    row = lax.broadcasted_iota(jnp.int32, (half, half), 0)
    column = lax.broadcasted_iota(jnp.int32, (half, half), 1)
    return row < column, row == column


def pack_kernel(odd, own_ref, other_ref, f_ref, all_ref):
    half = own_ref.shape[1]
    above, on = corner_masks(half)
    for s in range(STEPS):
        out_ref = all_ref.at[s]
        out_ref[:half, :] = own_ref[s]

        @pl.when(odd[s] == 1)
        def _():
            out_ref[:half, :] = other_ref[s]

        first = f_ref[s, :half, :half]
        second = f_ref[s, half:, half:]
        out_ref[half : 2 * half, :half] = jnp.where(above | on, first, second.T)
        out_ref[half : 2 * half, half:] = f_ref[s, :half, half:]
        diagonal = jnp.sum(jnp.where(on, second, 0.0), axis=0, keepdims=True)
        line = jnp.concatenate([diagonal, jnp.zeros_like(diagonal)], axis=1)
        out_ref[2 * half :, :] = jnp.broadcast_to(line, (8, 2 * half))


def pack(own, other, factors, odd):
    steps, half, panel = own.shape
    shape = (steps, panel + 8, panel)
    return pl.pallas_call(
        pack_kernel,
        out_shape=jax.ShapeDtypeStruct(shape, jnp.float32),
        grid_spec=pltpu.PrefetchScalarGridSpec(
            num_scalar_prefetch=1,
            grid=(1,),
            in_specs=[
                pl.BlockSpec(own.shape, lambda c, *_: (0, 0, 0)),
                pl.BlockSpec(other.shape, lambda c, *_: (0, 0, 0)),
                pl.BlockSpec(factors.shape, lambda c, *_: (0, 0, 0)),
            ],
            out_specs=pl.BlockSpec(shape, lambda c, *_: (0, 0, 0)),
        ),
    )(odd, own, other, factors)


def chip_at(place, chips):
    return jnp.where(place < chips // 2, 2 * place, 2 * (chips - 1 - place) + 1)


def place_of(chip, chips):
    return jnp.where(chip % 2 == 0, chip // 2, chips - 1 - chip // 2)


def leaf_block(listed, odd, m_ref, u_ref, out_ref, tops_ref, first, parts):
    yh, yl, yth, ytl, lth, ltl, uh, ul = parts
    panel = u_ref.shape[1]
    width = out_ref.shape[1]
    block_count = out_ref.shape[0] // BLK
    listed_count = yh.shape[1] // BLK
    panel_blocks = panel // BLK
    out_ref[...] = m_ref[...]
    for s in range(STEPS):
        inner = range((s + 1) * panel_blocks, block_count - 1)
        numbers = {
            k: jnp.full((BLK, width), listed[s, k], jnp.int32)
            for k in range(panel_blocks, listed_count - 1)
        }
        taken = [out_ref[s * panel : (s + 1) * panel, :]]
        for number in numbers.values():
            block_rows = jnp.zeros((BLK, width), jnp.float32)
            for block in inner:
                here = out_ref[block * BLK : (block + 1) * BLK, :]
                block_rows = jnp.where(number == block, here, block_rows)
            taken.append(block_rows)
        taken.append(out_ref[(block_count - 1) * BLK :, :])
        gathered = jnp.concatenate(taken, axis=0)
        projected = product3((yth[s], ytl[s]), split(gathered), NN)
        update = product3((lth[s], ltl[s]), split(projected), NN)
        change = product3((yh[s], yl[s]), split(update), NN)
        pieces = [change[k * BLK : (k + 1) * BLK] for k in range(listed_count)]
        fixed = [(s * panel_blocks + k, pieces[k]) for k in range(panel_blocks)]
        for block, piece in fixed + [(block_count - 1, pieces[-1])]:
            out_ref[block * BLK : (block + 1) * BLK, :] -= piece
        for block in inner:
            amount = jnp.zeros((BLK, width), jnp.float32)
            for k, number in numbers.items():
                amount = jnp.where(number == block, pieces[k], amount)
            out_ref[block * BLK : (block + 1) * BLK, :] -= amount
    for s in range(STEPS):
        turned = out_ref[s * panel : (s + 1) * panel, :].T
        projected = product3(split(turned), (uh[s], ul[s]), NN)
        flag = jnp.full(turned.shape, odd[s], jnp.int32)
        tops_ref[pl.ds(first, width), s * panel : (s + 1) * panel] = jnp.where(
            flag == 1, projected, turned
        )


def exchange_kernel(count, listed, odd, m_ref, y_ref, l_ref, u_ref, p_ref, work_ref, g_ref, r_ref, *rest):
    parts = rest[:8]
    t_ref, ring_send, ring_recv, pass_send, pass_recv, a2a_send, a2a_recv, own_sem = rest[8:]
    turn = pl.program_id(0)
    turns = t_ref.shape[0] // m_ref.shape[1]
    me = lax.axis_index("row")
    chips = count // 2
    share = t_ref.shape[0] // count
    core = me % 2
    place = place_of(me // 2, chips)

    def device(offset):
        return chip_at((place + offset + chips) % chips, chips) * 2 + core

    partner = me + 1 - 2 * core
    right, left = device(1), device(-1)

    def remote(source, target, send_sem, recv_sem, peer):
        return pltpu.make_async_remote_copy(
            src_ref=source,
            dst_ref=target,
            send_sem=send_sem,
            recv_sem=recv_sem,
            device_id={"row": peer},
            device_id_type=pl.DeviceIdType.MESH,
        )

    lengths = {(0, 0): chips // 2, (0, 1): chips - 1 - chips // 2}
    lengths[1, 1], lengths[1, 0] = lengths[0, 0], lengths[0, 1]
    longest = max(lengths.values())

    def hop(s, way, t):
        origin = device(-t if way == 0 else t)
        source = p_ref.at[s] if t == 0 else g_ref.at[origin, s]
        return remote(
            source,
            g_ref.at[origin, s],
            ring_send.at[s, way, t],
            ring_recv.at[s, way, t],
            right if way == 0 else left,
        )

    def hand(s, way, t):
        if t < 0:
            return remote(
                p_ref.at[s], g_ref.at[me, s], pass_send.at[s, 0], pass_recv.at[s, 0], partner
            )
        origin = device(-t - 1 if way == 0 else t + 1)
        slot = 1 + (t if way == 0 else lengths[s, 0] + t)
        piece = g_ref.at[origin, s]
        return remote(piece, piece, pass_send.at[s, slot], pass_recv.at[s, slot], partner)

    def columns_of(peer):
        return t_ref.at[pl.ds(pl.multiple_of(peer * share, 8), share), :]

    def scatter(j):
        peer = (me + j) % count
        return remote(columns_of(peer), r_ref.at[me], a2a_send.at[j - 1], a2a_recv.at[j - 1], peer)

    def keep(s):
        return pltpu.make_async_copy(p_ref.at[s], g_ref.at[me, s], own_sem.at[s])

    def keep_columns():
        return pltpu.make_async_copy(columns_of(me), r_ref.at[me], own_sem.at[STEPS])

    def advance(t):
        for s, way in lengths:
            if t < lengths[s, way]:
                hop(s, way, t).wait_recv()
                if t + 1 < lengths[s, way]:
                    hop(s, way, t + 1).start()
                hand(s, way, t).start()

    @pl.when(turn == 0)
    def _():
        barrier = pltpu.get_barrier_semaphore()
        for j in range(1, count):
            pl.semaphore_signal(
                barrier,
                inc=1,
                device_id={"row": (me + j) % count},
                device_id_type=pl.DeviceIdType.MESH,
            )
        pl.semaphore_wait(barrier, count - 1)
        for s, way in lengths:
            if lengths[s, way] > 0:
                hop(s, way, 0).start()
        for s in range(STEPS):
            hand(s, 0, -1).start()
            keep(s).start()
        yh, yl, yth, ytl, lth, ltl, uh, ul = parts
        for s in range(STEPS):
            yh[s], yl[s] = split(y_ref[s])
            yth[s], ytl[s] = split(y_ref[s].T)
            lth[s], ltl[s] = split(l_ref[s].T)
            uh[s], ul[s] = split(u_ref[s])

    first = pl.multiple_of(turn * m_ref.shape[1], m_ref.shape[1])
    leaf_block(listed, odd, m_ref, u_ref, work_ref, t_ref, first, parts)

    early = min(turns - 1, longest)
    for t in range(early):

        @pl.when(turn == t)
        def _():
            advance(t)

    @pl.when(turn == turns - 1)
    def _():
        todo = [(j + count // 2 - 1) % (count - 1) + 1 for j in range(count - 1)]
        rounds = max(longest - early, 1)
        size = -(-len(todo) // rounds)
        keep_columns().start()
        for t in range(rounds):
            for j in todo[t * size : (t + 1) * size]:
                scatter(j).start()
            advance(early + t)
        for s, way in lengths:
            for t in range(lengths[s, way]):
                hop(s, way, t).wait_send()
                hand(s, way, t).wait()
        for s in range(STEPS):
            hand(s, 0, -1).wait()
            keep(s).wait()
        keep_columns().wait()
        for j in todo:
            scatter(j).wait()


def exchange(count, matrix, leaf_vectors, leaf_factors, tree_vectors, packed, leaf_blocks, odd):
    rows, columns = matrix.shape
    width = COLS_PER_LEAF
    steps, leaf_rows, panel = leaf_vectors.shape
    chips = count // 2
    dma = pltpu.SemaphoreType.DMA
    half_type = jnp.bfloat16

    def whole(array):
        return pl.BlockSpec(array.shape, lambda c, *_: (0, 0, 0))

    return pl.pallas_call(
        functools.partial(exchange_kernel, count),
        out_shape=(
            jax.ShapeDtypeStruct((rows, columns), jnp.float32),
            jax.ShapeDtypeStruct((count,) + packed.shape, jnp.float32),
            jax.ShapeDtypeStruct((count, columns // count, steps * panel), jnp.float32),
        ),
        grid_spec=pltpu.PrefetchScalarGridSpec(
            num_scalar_prefetch=2,
            grid=(columns // width,),
            in_specs=[
                pl.BlockSpec((rows, width), lambda c, *_: (0, c)),
                whole(leaf_vectors),
                whole(leaf_factors),
                whole(tree_vectors),
                whole(packed),
            ],
            out_specs=[
                pl.BlockSpec((rows, width), lambda c, *_: (0, c)),
                pl.BlockSpec(memory_space=pl.ANY),
                pl.BlockSpec(memory_space=pl.ANY),
            ],
            scratch_shapes=[
                *[pltpu.VMEM((steps, leaf_rows, panel), half_type)] * 2,
                *[pltpu.VMEM((steps, panel, leaf_rows), half_type)] * 2,
                *[pltpu.VMEM((steps, panel, panel), half_type)] * 4,
                pltpu.VMEM((columns, steps * panel), jnp.float32),
                dma((steps, 2, chips)),
                dma((steps, 2, chips)),
                dma((steps, chips)),
                dma((steps, chips)),
                dma((count - 1,)),
                dma((count - 1,)),
                dma((steps + 1,)),
            ],
        ),
        compiler_params=pltpu.CompilerParams(collective_id=0, has_side_effects=True),
    )(leaf_blocks, odd, matrix, leaf_vectors, leaf_factors, tree_vectors, packed)


def tree_kernel(upper, lower, x_ref, g_ref, out_ref):
    node = pl.program_id(0)
    panel = g_ref.shape[2]
    half = panel // 2
    first_level = x_ref.shape[0] // 2

    @pl.when(node == 0)
    def _():
        out_ref[...] = x_ref[...]

    a, b = upper[node], lower[node]
    slot = lax.rem(b, 2)
    above, on = corner_masks(half)
    corner = g_ref[slot, half : 2 * half, :half]
    diagonal = g_ref[slot, 2 * half : 2 * half + 1, :half]
    top = jnp.concatenate(
        [jnp.where(above | on, corner, 0.0), g_ref[slot, half : 2 * half, half:]], axis=1
    )
    last = jnp.where(above, corner.T, jnp.where(on, diagonal, 0.0))
    bottom = jnp.concatenate([jnp.zeros_like(last), last], axis=1)
    f = split(jnp.concatenate([top, bottom], axis=0))
    xa, xb = out_ref[a], out_ref[b]

    @pl.when(node < first_level)
    def _():
        w = product3(split(xa + xb), f, NN)
        out_ref[a] = xa - w
        out_ref[b] = w

    @pl.when(node >= first_level)
    def _():
        u = split(jnp.concatenate([g_ref[0, :half, :], g_ref[1, :half, :]], axis=0))
        w = product3(split(xa + product3(split(xb), u, NN)), f, NN)
        out_ref[a] = xa - w
        out_ref[b] = xb - product3(split(w), u, NT)


def tree(step, spread, reflectors, upper, lower):
    devices, width, both = spread.shape
    block = (devices, width, both // STEPS)
    return pl.pallas_call(
        tree_kernel,
        out_shape=jax.ShapeDtypeStruct(block, jnp.float32),
        grid_spec=pltpu.PrefetchScalarGridSpec(
            num_scalar_prefetch=2,
            grid=(devices - 1,),
            in_specs=[
                pl.BlockSpec(block, lambda n, *_: (0, 0, step)),
                pl.BlockSpec(
                    (2, None) + reflectors.shape[2:], lambda n, up, lo: (lo[n] // 2, step, 0, 0)
                ),
            ],
            out_specs=pl.BlockSpec(block, lambda n, *_: (0, 0, 0)),
        ),
    )(upper, lower, spread, reflectors)


def place_rows(flag, back_ref, u_ref, rows_ref, out_ref):
    @pl.when(flag == 0)
    def _():
        out_ref[...] = back_ref[...].T

    @pl.when(flag == 1)
    def _():
        out_ref[...] = rows_ref[...] - product3(split(u_ref[...]), split(back_ref[...]), NT)


def place_kernel(odd, back_ref, u_ref, work_ref, out_ref):
    panel = u_ref.shape[0]
    rows = out_ref.shape[0]
    place_rows(odd[0], back_ref, u_ref, work_ref.at[:panel], out_ref.at[:panel])
    if rows > panel:
        out_ref[panel:, :] = work_ref[panel:, :]


def place(step, back, vectors, work, odd):
    columns, panel = back.shape
    width = COLS_PER_LEAF
    rows = work.shape[0] if step == 0 else panel
    return pl.pallas_call(
        place_kernel,
        out_shape=jax.ShapeDtypeStruct(work.shape, jnp.float32),
        grid_spec=pltpu.PrefetchScalarGridSpec(
            num_scalar_prefetch=1,
            grid=(columns // width,),
            in_specs=[
                pl.BlockSpec((width, panel), lambda c, *_: (c, 0)),
                pl.BlockSpec((panel, panel), lambda c, *_: (0, 0)),
                pl.BlockSpec((rows, width), lambda c, *_: (step, c)),
            ],
            out_specs=pl.BlockSpec((rows, width), lambda c, *_: (step, c)),
        ),
        input_output_aliases={} if step == 0 else {3: 0},
    )(odd, back, vectors, work)


def pairs(row_count):
    uppers, lowers = [], []
    gap = 1
    while gap < row_count:
        for start in range(0, row_count, 2 * gap):
            uppers.append(start)
            lowers.append(start + gap)
        gap *= 2
    return jnp.array(uppers, jnp.int32), jnp.array(lowers, jnp.int32)


def spread_shards(matrix, leaf_vectors, leaf_factors, tree_vectors, tree_factors, leaf_blocks, owner):
    row_count = lax.axis_size("row")
    my_index = lax.axis_index("row")
    columns = matrix.shape[1]
    panel = tree_vectors.shape[2]
    half = panel // 2
    core = my_index % 2
    odd = ((my_index - owner) % 2).astype(jnp.int32)
    own = lax.dynamic_slice_in_dim(tree_vectors, core * half, half, axis=1)
    asked = lax.dynamic_slice_in_dim(tree_vectors, (1 - core) * half, half, axis=1)
    other = lax.ppermute(asked, "row", [(i, i ^ 1) for i in range(row_count)])
    packed = pack(own, other, tree_factors, odd)
    work, reflectors, spread = exchange(
        row_count, matrix, leaf_vectors, leaf_factors, tree_vectors, packed, leaf_blocks, odd
    )
    uppers, lowers = pairs(row_count)
    for s in range(STEPS):
        upper, lower = (uppers + owner[s]) % row_count, (lowers + owner[s]) % row_count
        done = tree(s, spread, reflectors, upper, lower)
        back = lax.all_to_all(done, "row", 0, 0).reshape(columns, panel)
        work = place(s, back, tree_vectors[s], work, odd[s : s + 1])
    return work


def plan(count):
    half = count // 2
    rows = []
    for owner in range(count):
        edges = []
        gap = 1
        while gap < count:
            for p in range(0, count, 2 * gap):
                edges.append((gap, (p + owner) % count, (p + gap + owner) % count))
            gap *= 2
        blocked = [False] * count
        inner, outer = ([], []), []
        for gap, a, b in edges:
            if a // half == b // half and not (blocked[a] or blocked[b]):
                inner[a // half].append((gap, a, b))
            else:
                outer.append((gap, a, b))
                blocked[a] = blocked[b] = True
        active = [[i for i in range(count) if blocked[i] and i // half == h] for h in (0, 1)]
        for h in (0, 1):
            where = {half * h + t: t for t in range(half)}
            row = []

            def emit(chosen, places, base):
                entries = [(0, 0, 0)] * len(places)
                used = set()
                for gap, a, b in chosen:
                    k = next(k for k, g in enumerate(places) if k not in used and g in (0, gap))
                    used.add(k)
                    entries[k] = (where[a], where[b], b // 2)
                    where[a], where[b] = base + 2 * k, base + 2 * k + 1
                for entry in entries:
                    row.extend(entry)

            emit([e for e in inner[h] if e[0] == 1], HALF_ODD, half)
            emit([e for e in inner[h] if e[0] > 1], HALF_EVEN, half + 2 * len(HALF_ODD))
            slots = [where[i] for i in active[h]]
            row.extend(slots + [0] * (SLOTS - len(slots)))
            base = half + 2 * len(HALF_ODD) + 2 * len(HALF_EVEN)
            for side in (0, 1):
                for k, i in enumerate(active[h ^ side]):
                    where[i] = base + SLOTS * side + k
            base += 2 * SLOTS
            emit([e for e in outer if e[0] == 1], TOP_ODD, base)
            emit([e for e in outer if e[0] > 1], TOP_EVEN, base + 2 * len(TOP_ODD))
            row.extend(where[half * h + t] for t in range(half))
            rows.append(row)
    return np.array(rows, np.int32)


def tree_product(operators, index, right):
    high, low = operators
    return product3((high[index], low[index]), split(right), NN)


def pipeline_kernel(
    count, turns, listed, owner, table, m_ref, y_ref, l_ref, u_ref, f_ref, tops_ref, low_ref, *scratch
):
    (
        yh, yl, yth, ytl, lth, ltl, uh, ul, uth, utl,
        wk, home, out_tops, in_tops, values, out_slots, in_slots, out_done, in_done,
        raw, mine, packs,
        foh, fol, feh, fel, tuh, tul, tth, ttl,
        raw_send, raw_recv, pack_send, pack_recv, pass_send,
        tops_send, tops_recv, slots_send, slots_recv, done_send, done_recv,
    ) = scratch
    step_now = pl.program_id(0)
    half = count // 2
    chips = count // 2
    panel = u_ref.shape[1]
    width = m_ref.shape[1]
    part = width // 2
    block_count = m_ref.shape[0] // BLK
    listed_count = y_ref.shape[1] // BLK
    panel_blocks = panel // BLK
    me = lax.axis_index("row")
    side = me // half
    local = me % half
    chip = me // 2
    core = me % 2
    partner = me + 1 - 2 * core
    holds = (me >= half // 2) & (me < half + half // 2)
    my_step = chip % 2
    across = me + half // 2 - half * side
    primary = holds & (core == my_step)
    row_length = table.shape[0] // (2 * count)

    def remote(source, target, send_sem, recv_sem, peer):
        return pltpu.make_async_remote_copy(
            src_ref=source,
            dst_ref=target,
            send_sem=send_sem,
            recv_sem=recv_sem,
            device_id={"row": peer},
            device_id_type=pl.DeviceIdType.MESH,
        )

    def holder(h, s, j):
        return half // 2 * (1 + h) + 2 * s + j

    def send_raw(k):
        source = (u_ref if k == 0 else f_ref).at[1 - core]
        return remote(source, raw.at[k], raw_send.at[k], raw_recv.at[k], partner)

    def send_pack(h):
        return remote(mine, packs.at[chip], pack_send.at[h], pack_recv.at[chip], holder(h, core, core))

    def receive_pack(c):
        return remote(packs.at[c], packs.at[c], pass_send.at[c], pack_recv.at[c], partner)

    def send_tops(t, s, j):
        return remote(
            out_tops.at[t, s, j], in_tops.at[t, local], tops_send.at[t, 2 * s + j],
            tops_recv.at[t, local], holder(side, s, j),
        )

    def receive_tops(t, source):
        return remote(
            in_tops.at[t, source], in_tops.at[t, source], tops_send.at[t, 0],
            tops_recv.at[t, source], across,
        )

    def send_slots(t):
        return remote(out_slots.at[t], in_slots.at[t], slots_send.at[t], slots_recv.at[t], across)

    def send_done(t, target):
        return remote(
            out_done.at[t, target], in_done.at[t, 2 * my_step + core], done_send.at[t, target],
            done_recv.at[t, 2 * my_step + core], half * side + target,
        )

    def receive_done(t, k):
        return remote(
            in_done.at[t, k], in_done.at[t, k], done_send.at[t, 0], done_recv.at[t, k], across
        )

    def flag(value, shape):
        return jnp.full(shape, value, jnp.int32) == 1

    def odd(s):
        return (me + count - owner[s]) % 2

    square = (panel, panel)

    @pl.when(step_now == 0)
    def _():
        barrier = pltpu.get_barrier_semaphore()
        for j in range(1, count):
            pl.semaphore_signal(
                barrier,
                inc=1,
                device_id={"row": (me + j) % count},
                device_id_type=pl.DeviceIdType.MESH,
            )
        pl.semaphore_wait(barrier, count - 1)
        for k in range(2):
            send_raw(k).start()
        for s in range(STEPS):
            yh[s], yl[s] = split(y_ref[s])
            yth[s], ytl[s] = split(y_ref[s].T)
            lth[s], ltl[s] = split(l_ref[s].T)
            uh[s], ul[s] = split(u_ref[s])
            uth[s], utl[s] = split(u_ref[s].T)
        for k in range(2):
            send_raw(k).wait_recv()
        even = 1 - jnp.where(core == 0, odd(0), odd(1))
        mine[:panel, :] = jnp.where(flag(even, square), u_ref[core], raw[0])
        own, other = f_ref[core], raw[1]
        fe = jnp.where(flag(even, square), own, other)
        fo = jnp.where(flag(even, square), other, own)
        row = lax.broadcasted_iota(jnp.int32, square, 0)
        column = lax.broadcasted_iota(jnp.int32, square, 1)
        mine[panel : 2 * panel, :] = jnp.where(row <= column, fe, fo.T)
        diagonal = jnp.sum(jnp.where(row == column, fo, 0.0), axis=0, keepdims=True)
        mine[2 * panel :, :] = jnp.broadcast_to(diagonal, (8, panel))
        for d in range(2):
            h = (side + d) % 2

            @pl.when(holder(h, core, core) == me)
            def _():
                packs[chip] = mine[...]

            @pl.when(holder(h, core, core) != me)
            def _():
                send_pack(h).start()

    def unpack(h):
        def one(q, carry):
            c = h * (chips // 2) + q
            own = c == chip

            @pl.when(jnp.logical_not(primary & own))
            def _():
                receive_pack(c).wait_recv()

            @pl.when(primary)
            def _():
                receive_pack(c).start()

            u = packs[c, :panel, :]
            f = packs[c, panel : 2 * panel, :]
            diagonal = packs[c, 2 * panel : 2 * panel + 1, :]
            row = lax.broadcasted_iota(jnp.int32, square, 0)
            column = lax.broadcasted_iota(jnp.int32, square, 1)
            foh[c], fol[c] = split(
                jnp.where(row > column, f, jnp.where(row == column, diagonal, 0.0))
            )
            feh[c], fel[c] = split(jnp.where(row <= column, f, 0.0).T)
            tuh[c], tul[c] = split(u)
            tth[c], ttl[c] = split(u.T)
            return carry

        lax.fori_loop(0, chips // 2, one, 0)

    def leaf(t):
        for b in range(block_count):
            wk[b] = m_ref[b * BLK : (b + 1) * BLK, :]
        for s in range(STEPS):
            inner = range((s + 1) * panel_blocks, block_count - 1)
            numbers = range(panel_blocks, listed_count - 1)
            taken = [wk[s * panel_blocks + k] for k in range(panel_blocks)]
            taken += [wk[listed[s, k]] for k in numbers]
            taken.append(wk[block_count - 1])
            gathered = jnp.concatenate(taken, axis=0)
            projected = product3((yth[s], ytl[s]), split(gathered), NN)
            update = product3((lth[s], ltl[s]), split(projected), NN)
            change = product3((yh[s], yl[s]), split(update), NN)
            pieces = [change[k * BLK : (k + 1) * BLK] for k in range(listed_count)]
            wk[block_count - 1] -= pieces[-1]
            for block in inner:
                amount = jnp.zeros((BLK, width), jnp.float32)
                for k in numbers:
                    number = jnp.full((BLK, width), listed[s, k], jnp.int32)
                    amount = jnp.where(number == block, pieces[k], amount)
                wk[block] -= amount
            tops = [taken[k] - pieces[k] for k in range(panel_blocks)]
            tops = jnp.concatenate(tops, axis=0)
            home[t, s] = tops
            projected = product3((uth[s], utl[s]), split(tops), NN)
            tops = jnp.where(flag(odd(s), (panel, width)), projected, tops)
            for j in range(2):
                piece = tops[:, j * part : (j + 1) * part]
                out_tops[t, s, j] = piece

                @pl.when(holder(side, s, j) == me)
                def _():
                    in_tops[t, local] = piece

                @pl.when(holder(side, s, j) != me)
                def _():
                    send_tops(t, s, j).start()

        for b in range(STEPS * panel_blocks, block_count):
            first = (b - STEPS * panel_blocks) * BLK
            low_ref[first : first + BLK, :] = wk[b]

    start_of_row = (jnp.where(my_step == 0, owner[0], owner[1]) * 2 + side) * row_length

    def entry(k):
        return table[start_of_row + k]

    def pairs_of(first, places, base, even):
        for k in range(len(places)):
            a, b = values[entry(first + 3 * k)], values[entry(first + 3 * k + 1)]
            c = entry(first + 3 * k + 2)
            if even:
                w = tree_product((feh, fel), c, a + tree_product((tth, ttl), c, b))
                lower = b - tree_product((tuh, tul), c, w)
            else:
                w = lower = tree_product((foh, fol), c, a + b)
            values[base + 2 * k] = a - w
            values[base + 2 * k + 1] = lower
        return first + 3 * len(places), base + 2 * len(places)

    half_entries = 3 * (len(HALF_ODD) + len(HALF_EVEN))
    slots_at = half + 2 * (len(HALF_ODD) + len(HALF_EVEN))
    top_entries = half_entries + SLOTS
    done_entries = top_entries + 3 * (len(TOP_ODD) + len(TOP_EVEN))

    def half_tree(t):
        for source in range(half):

            @pl.when(source != local)
            def _():
                receive_tops(t, source).wait_recv()

            values[source] = in_tops[t, source]
        first, base = pairs_of(0, HALF_ODD, half, False)
        pairs_of(first, HALF_EVEN, base, True)
        for k in range(SLOTS):
            block = values[entry(half_entries + k)]
            values[slots_at + k] = block
            out_slots[t, k] = block
        send_slots(t).start()

    def top_tree(t):
        send_slots(t).wait_recv()
        for k in range(SLOTS):
            values[slots_at + SLOTS + k] = in_slots[t, k]
        first, base = pairs_of(top_entries, TOP_ODD, slots_at + 2 * SLOTS, False)
        pairs_of(first, TOP_EVEN, base, True)
        for target in range(half):
            block = values[entry(done_entries + target)]
            out_done[t, target] = block

            @pl.when(target == local)
            def _():
                in_done[t, 2 * my_step + core] = block

            @pl.when(target != local)
            def _():
                send_done(t, target).start()

    def place_tops(t):
        for s in range(STEPS):
            for j in range(2):

                @pl.when(holder(side, s, j) != me)
                def _():
                    receive_done(t, 2 * s + j).wait_recv()

            back = jnp.concatenate([in_done[t, 2 * s], in_done[t, 2 * s + 1]], axis=1)
            lower = home[t, s] - product3((uh[s], ul[s]), split(back), NN)
            tops_ref[s * panel : (s + 1) * panel, :] = jnp.where(
                flag(odd(s), (panel, width)), lower, back
            )

    @pl.when(step_now < turns)
    def _():
        leaf(step_now)

    for d in range(2):

        @pl.when(holds & (step_now == 1 + d))
        def _():
            unpack((side + d) % 2)

        if d == 1:

            @pl.when(holds & (step_now >= 2) & (step_now < turns + 2))
            def _():
                top_tree(step_now - 2)

    @pl.when(holds & (step_now >= 1) & (step_now < turns + 1))
    def _():
        half_tree(step_now - 1)

    @pl.when(step_now >= 3)
    def _():
        place_tops(step_now - 3)

    @pl.when(step_now == turns + 2)
    def _():
        for k in range(2):
            send_raw(k).wait_send()
        for h in range(2):

            @pl.when(holder(h, core, core) != me)
            def _():
                send_pack(h).wait_send()

        @pl.when(primary)
        def _():
            for c in range(chips):
                receive_pack(c).wait_send()

        for t in range(turns):
            for s in range(STEPS):
                for j in range(2):

                    @pl.when(holder(side, s, j) != me)
                    def _():
                        send_tops(t, s, j).wait_send()

        @pl.when(holds)
        def _():
            for t in range(turns):
                send_slots(t).wait_send()
                for target in range(half):

                    @pl.when(target != local)
                    def _():
                        send_done(t, target).wait_send()


def pipeline(count, matrix, leaf_vectors, leaf_factors, tree_vectors, tree_factors, leaf_blocks, owner):
    rows, columns = matrix.shape
    width = COLS_PER_LEAF
    part = width // 2
    steps, leaf_rows, panel = leaf_vectors.shape
    turns = columns // width
    half = count // 2
    chips = count // 2
    dma = pltpu.SemaphoreType.DMA
    short = jnp.bfloat16
    top_rows = steps * panel
    lag = 3
    value_count = half + 2 * (len(HALF_ODD) + len(HALF_EVEN) + SLOTS + len(TOP_ODD) + len(TOP_EVEN))
    block = (panel, part)

    def vmem(*shape):
        return pltpu.VMEM(shape, jnp.float32)

    def whole(array):
        return pl.BlockSpec(array.shape, lambda c, *_: (0, 0, 0), pipeline_mode=pl.Buffered(1))

    tops, low = pl.pallas_call(
        functools.partial(pipeline_kernel, count, turns),
        out_shape=(
            jax.ShapeDtypeStruct((top_rows, columns), jnp.float32),
            jax.ShapeDtypeStruct((rows - top_rows, columns), jnp.float32),
        ),
        grid_spec=pltpu.PrefetchScalarGridSpec(
            num_scalar_prefetch=3,
            grid=(turns + lag,),
            in_specs=[
                pl.BlockSpec((rows, width), lambda c, *_: (0, jnp.minimum(c, turns - 1))),
                whole(leaf_vectors),
                whole(leaf_factors),
                whole(tree_vectors),
                whole(tree_factors),
            ],
            out_specs=[
                pl.BlockSpec((top_rows, width), lambda c, *_: (0, jnp.maximum(c - lag, 0))),
                pl.BlockSpec((rows - top_rows, width), lambda c, *_: (0, jnp.minimum(c, turns - 1))),
            ],
            scratch_shapes=[
                *[pltpu.VMEM((steps, leaf_rows, panel), short)] * 2,
                *[pltpu.VMEM((steps, panel, leaf_rows), short)] * 2,
                *[pltpu.VMEM((steps, panel, panel), short)] * 6,
                vmem(rows // BLK, BLK, width),
                vmem(turns, steps, panel, width),
                vmem(turns, steps, 2, *block),
                vmem(turns, half, *block),
                vmem(value_count, *block),
                vmem(turns, SLOTS, *block),
                vmem(turns, SLOTS, *block),
                vmem(turns, half, *block),
                vmem(turns, 2 * steps, *block),
                vmem(2, panel, panel),
                vmem(2 * panel + 8, panel),
                vmem(chips, 2 * panel + 8, panel),
                *[pltpu.VMEM((chips, panel, panel), short)] * 8,
                dma((2,)),
                dma((2,)),
                dma((2,)),
                dma((chips,)),
                dma((chips,)),
                dma((turns, 2 * steps)),
                dma((turns, half)),
                dma((turns,)),
                dma((turns,)),
                dma((turns, half)),
                dma((turns, 2 * steps)),
            ],
        ),
        compiler_params=pltpu.CompilerParams(
            collective_id=0, has_side_effects=True, vmem_limit_bytes=60 * 2**20
        ),
    )(
        leaf_blocks, owner, jnp.asarray(plan(count).reshape(-1)),
        matrix, leaf_vectors, leaf_factors, tree_vectors, tree_factors,
    )
    return jnp.concatenate([tops, low], axis=0)


def shards(*arrays):
    row_count = lax.axis_size("row")
    if row_count == PLANNED_ROWS:
        return pipeline(row_count, *arrays)
    return spread_shards(*arrays)


def solution(mesh):
    return jax.shard_map(
        shards,
        mesh=mesh,
        in_specs=(
            P(("groups", "row"), None),
            P("groups", "row", None),
            P("groups", "row", None),
            P("groups", "row", None),
            P("groups", "row", None),
            P("groups", "row"),
            P("groups"),
        ),
        out_specs=P(("groups", "row"), None),
        check_vma=False,
    )
```

```python
import functools

import jax
import jax.numpy as jnp
import numpy as np
from jax import lax
from jax.experimental import pallas as pl
from jax.experimental.pallas import tpu as pltpu
from jax.sharding import PartitionSpec as P

BLK = 128
STEPS = 2
COLS_PER_LEAF = 256

PLANNED_ROWS = 16
HALF_ODD = (1, 1, 1, 1)
HALF_EVEN = (2, 2, 4)
TOP_ODD = (1, 1)
TOP_EVEN = (2, 2, 4, 4, 8)
SLOTS = 4

NN = (((1,), (0,)), ((), ()))
TN = (((0,), (0,)), ((), ()))
NT = (((1,), (1,)), ((), ()))


def split(value):
    high = value.astype(jnp.bfloat16)
    low = (value - high.astype(jnp.float32)).astype(jnp.bfloat16)
    return high, low


def product3(left, right, dims):
    def one(a, b):
        return lax.dot_general(a, b, dims, preferred_element_type=jnp.float32)

    return one(left[0], right[0]) + (one(left[0], right[1]) + one(left[1], right[0]))


def corner_masks(half):
    row = lax.broadcasted_iota(jnp.int32, (half, half), 0)
    column = lax.broadcasted_iota(jnp.int32, (half, half), 1)
    return row < column, row == column


def pack_kernel(odd, own_ref, other_ref, f_ref, all_ref):
    half = own_ref.shape[1]
    above, on = corner_masks(half)
    for s in range(STEPS):
        out_ref = all_ref.at[s]
        out_ref[:half, :] = own_ref[s]

        @pl.when(odd[s] == 1)
        def _():
            out_ref[:half, :] = other_ref[s]

        first = f_ref[s, :half, :half]
        second = f_ref[s, half:, half:]
        out_ref[half : 2 * half, :half] = jnp.where(above | on, first, second.T)
        out_ref[half : 2 * half, half:] = f_ref[s, :half, half:]
        diagonal = jnp.sum(jnp.where(on, second, 0.0), axis=0, keepdims=True)
        line = jnp.concatenate([diagonal, jnp.zeros_like(diagonal)], axis=1)
        out_ref[2 * half :, :] = jnp.broadcast_to(line, (8, 2 * half))


def pack(own, other, factors, odd):
    steps, half, panel = own.shape
    shape = (steps, panel + 8, panel)
    return pl.pallas_call(
        pack_kernel,
        out_shape=jax.ShapeDtypeStruct(shape, jnp.float32),
        grid_spec=pltpu.PrefetchScalarGridSpec(
            num_scalar_prefetch=1,
            grid=(1,),
            in_specs=[
                pl.BlockSpec(own.shape, lambda c, *_: (0, 0, 0)),
                pl.BlockSpec(other.shape, lambda c, *_: (0, 0, 0)),
                pl.BlockSpec(factors.shape, lambda c, *_: (0, 0, 0)),
            ],
            out_specs=pl.BlockSpec(shape, lambda c, *_: (0, 0, 0)),
        ),
    )(odd, own, other, factors)


def chip_at(place, chips):
    return jnp.where(place < chips // 2, 2 * place, 2 * (chips - 1 - place) + 1)


def place_of(chip, chips):
    return jnp.where(chip % 2 == 0, chip // 2, chips - 1 - chip // 2)


def leaf_block(listed, odd, m_ref, u_ref, out_ref, tops_ref, first, parts):
    yh, yl, yth, ytl, lth, ltl, uh, ul = parts
    panel = u_ref.shape[1]
    width = out_ref.shape[1]
    block_count = out_ref.shape[0] // BLK
    listed_count = yh.shape[1] // BLK
    panel_blocks = panel // BLK
    out_ref[...] = m_ref[...]
    for s in range(STEPS):
        inner = range((s + 1) * panel_blocks, block_count - 1)
        numbers = {
            k: jnp.full((BLK, width), listed[s, k], jnp.int32)
            for k in range(panel_blocks, listed_count - 1)
        }
        taken = [out_ref[s * panel : (s + 1) * panel, :]]
        for number in numbers.values():
            block_rows = jnp.zeros((BLK, width), jnp.float32)
            for block in inner:
                here = out_ref[block * BLK : (block + 1) * BLK, :]
                block_rows = jnp.where(number == block, here, block_rows)
            taken.append(block_rows)
        taken.append(out_ref[(block_count - 1) * BLK :, :])
        gathered = jnp.concatenate(taken, axis=0)
        projected = product3((yth[s], ytl[s]), split(gathered), NN)
        update = product3((lth[s], ltl[s]), split(projected), NN)
        change = product3((yh[s], yl[s]), split(update), NN)
        pieces = [change[k * BLK : (k + 1) * BLK] for k in range(listed_count)]
        fixed = [(s * panel_blocks + k, pieces[k]) for k in range(panel_blocks)]
        for block, piece in fixed + [(block_count - 1, pieces[-1])]:
            out_ref[block * BLK : (block + 1) * BLK, :] -= piece
        for block in inner:
            amount = jnp.zeros((BLK, width), jnp.float32)
            for k, number in numbers.items():
                amount = jnp.where(number == block, pieces[k], amount)
            out_ref[block * BLK : (block + 1) * BLK, :] -= amount
    for s in range(STEPS):
        turned = out_ref[s * panel : (s + 1) * panel, :].T
        projected = product3(split(turned), (uh[s], ul[s]), NN)
        flag = jnp.full(turned.shape, odd[s], jnp.int32)
        tops_ref[pl.ds(first, width), s * panel : (s + 1) * panel] = jnp.where(
            flag == 1, projected, turned
        )


def exchange_kernel(count, listed, odd, m_ref, y_ref, l_ref, u_ref, p_ref, work_ref, g_ref, r_ref, *rest):
    parts = rest[:8]
    t_ref, ring_send, ring_recv, pass_send, pass_recv, a2a_send, a2a_recv, own_sem = rest[8:]
    turn = pl.program_id(0)
    turns = t_ref.shape[0] // m_ref.shape[1]
    me = lax.axis_index("row")
    chips = count // 2
    share = t_ref.shape[0] // count
    core = me % 2
    place = place_of(me // 2, chips)

    def device(offset):
        return chip_at((place + offset + chips) % chips, chips) * 2 + core

    partner = me + 1 - 2 * core
    right, left = device(1), device(-1)

    def remote(source, target, send_sem, recv_sem, peer):
        return pltpu.make_async_remote_copy(
            src_ref=source,
            dst_ref=target,
            send_sem=send_sem,
            recv_sem=recv_sem,
            device_id={"row": peer},
            device_id_type=pl.DeviceIdType.MESH,
        )

    lengths = {(0, 0): chips // 2, (0, 1): chips - 1 - chips // 2}
    lengths[1, 1], lengths[1, 0] = lengths[0, 0], lengths[0, 1]
    longest = max(lengths.values())

    def hop(s, way, t):
        origin = device(-t if way == 0 else t)
        source = p_ref.at[s] if t == 0 else g_ref.at[origin, s]
        return remote(
            source,
            g_ref.at[origin, s],
            ring_send.at[s, way, t],
            ring_recv.at[s, way, t],
            right if way == 0 else left,
        )

    def hand(s, way, t):
        if t < 0:
            return remote(
                p_ref.at[s], g_ref.at[me, s], pass_send.at[s, 0], pass_recv.at[s, 0], partner
            )
        origin = device(-t - 1 if way == 0 else t + 1)
        slot = 1 + (t if way == 0 else lengths[s, 0] + t)
        piece = g_ref.at[origin, s]
        return remote(piece, piece, pass_send.at[s, slot], pass_recv.at[s, slot], partner)

    def columns_of(peer):
        return t_ref.at[pl.ds(pl.multiple_of(peer * share, 8), share), :]

    def scatter(j):
        peer = (me + j) % count
        return remote(columns_of(peer), r_ref.at[me], a2a_send.at[j - 1], a2a_recv.at[j - 1], peer)

    def keep(s):
        return pltpu.make_async_copy(p_ref.at[s], g_ref.at[me, s], own_sem.at[s])

    def keep_columns():
        return pltpu.make_async_copy(columns_of(me), r_ref.at[me], own_sem.at[STEPS])

    def advance(t):
        for s, way in lengths:
            if t < lengths[s, way]:
                hop(s, way, t).wait_recv()
                if t + 1 < lengths[s, way]:
                    hop(s, way, t + 1).start()
                hand(s, way, t).start()

    @pl.when(turn == 0)
    def _():
        barrier = pltpu.get_barrier_semaphore()
        for j in range(1, count):
            pl.semaphore_signal(
                barrier,
                inc=1,
                device_id={"row": (me + j) % count},
                device_id_type=pl.DeviceIdType.MESH,
            )
        pl.semaphore_wait(barrier, count - 1)
        for s, way in lengths:
            if lengths[s, way] > 0:
                hop(s, way, 0).start()
        for s in range(STEPS):
            hand(s, 0, -1).start()
            keep(s).start()
        yh, yl, yth, ytl, lth, ltl, uh, ul = parts
        for s in range(STEPS):
            yh[s], yl[s] = split(y_ref[s])
            yth[s], ytl[s] = split(y_ref[s].T)
            lth[s], ltl[s] = split(l_ref[s].T)
            uh[s], ul[s] = split(u_ref[s])

    first = pl.multiple_of(turn * m_ref.shape[1], m_ref.shape[1])
    leaf_block(listed, odd, m_ref, u_ref, work_ref, t_ref, first, parts)

    early = min(turns - 1, longest)
    for t in range(early):

        @pl.when(turn == t)
        def _():
            advance(t)

    @pl.when(turn == turns - 1)
    def _():
        todo = [(j + count // 2 - 1) % (count - 1) + 1 for j in range(count - 1)]
        rounds = max(longest - early, 1)
        size = -(-len(todo) // rounds)
        keep_columns().start()
        for t in range(rounds):
            for j in todo[t * size : (t + 1) * size]:
                scatter(j).start()
            advance(early + t)
        for s, way in lengths:
            for t in range(lengths[s, way]):
                hop(s, way, t).wait_send()
                hand(s, way, t).wait()
        for s in range(STEPS):
            hand(s, 0, -1).wait()
            keep(s).wait()
        keep_columns().wait()
        for j in todo:
            scatter(j).wait()


def exchange(count, matrix, leaf_vectors, leaf_factors, tree_vectors, packed, leaf_blocks, odd):
    rows, columns = matrix.shape
    width = COLS_PER_LEAF
    steps, leaf_rows, panel = leaf_vectors.shape
    chips = count // 2
    dma = pltpu.SemaphoreType.DMA
    half_type = jnp.bfloat16

    def whole(array):
        return pl.BlockSpec(array.shape, lambda c, *_: (0, 0, 0))

    return pl.pallas_call(
        functools.partial(exchange_kernel, count),
        out_shape=(
            jax.ShapeDtypeStruct((rows, columns), jnp.float32),
            jax.ShapeDtypeStruct((count,) + packed.shape, jnp.float32),
            jax.ShapeDtypeStruct((count, columns // count, steps * panel), jnp.float32),
        ),
        grid_spec=pltpu.PrefetchScalarGridSpec(
            num_scalar_prefetch=2,
            grid=(columns // width,),
            in_specs=[
                pl.BlockSpec((rows, width), lambda c, *_: (0, c)),
                whole(leaf_vectors),
                whole(leaf_factors),
                whole(tree_vectors),
                whole(packed),
            ],
            out_specs=[
                pl.BlockSpec((rows, width), lambda c, *_: (0, c)),
                pl.BlockSpec(memory_space=pl.ANY),
                pl.BlockSpec(memory_space=pl.ANY),
            ],
            scratch_shapes=[
                *[pltpu.VMEM((steps, leaf_rows, panel), half_type)] * 2,
                *[pltpu.VMEM((steps, panel, leaf_rows), half_type)] * 2,
                *[pltpu.VMEM((steps, panel, panel), half_type)] * 4,
                pltpu.VMEM((columns, steps * panel), jnp.float32),
                dma((steps, 2, chips)),
                dma((steps, 2, chips)),
                dma((steps, chips)),
                dma((steps, chips)),
                dma((count - 1,)),
                dma((count - 1,)),
                dma((steps + 1,)),
            ],
        ),
        compiler_params=pltpu.CompilerParams(collective_id=0, has_side_effects=True),
    )(leaf_blocks, odd, matrix, leaf_vectors, leaf_factors, tree_vectors, packed)


def tree_kernel(upper, lower, x_ref, g_ref, out_ref):
    node = pl.program_id(0)
    panel = g_ref.shape[2]
    half = panel // 2
    first_level = x_ref.shape[0] // 2

    @pl.when(node == 0)
    def _():
        out_ref[...] = x_ref[...]

    a, b = upper[node], lower[node]
    slot = lax.rem(b, 2)
    above, on = corner_masks(half)
    corner = g_ref[slot, half : 2 * half, :half]
    diagonal = g_ref[slot, 2 * half : 2 * half + 1, :half]
    top = jnp.concatenate(
        [jnp.where(above | on, corner, 0.0), g_ref[slot, half : 2 * half, half:]], axis=1
    )
    last = jnp.where(above, corner.T, jnp.where(on, diagonal, 0.0))
    bottom = jnp.concatenate([jnp.zeros_like(last), last], axis=1)
    f = split(jnp.concatenate([top, bottom], axis=0))
    xa, xb = out_ref[a], out_ref[b]

    @pl.when(node < first_level)
    def _():
        w = product3(split(xa + xb), f, NN)
        out_ref[a] = xa - w
        out_ref[b] = w

    @pl.when(node >= first_level)
    def _():
        u = split(jnp.concatenate([g_ref[0, :half, :], g_ref[1, :half, :]], axis=0))
        w = product3(split(xa + product3(split(xb), u, NN)), f, NN)
        out_ref[a] = xa - w
        out_ref[b] = xb - product3(split(w), u, NT)


def tree(step, spread, reflectors, upper, lower):
    devices, width, both = spread.shape
    block = (devices, width, both // STEPS)
    return pl.pallas_call(
        tree_kernel,
        out_shape=jax.ShapeDtypeStruct(block, jnp.float32),
        grid_spec=pltpu.PrefetchScalarGridSpec(
            num_scalar_prefetch=2,
            grid=(devices - 1,),
            in_specs=[
                pl.BlockSpec(block, lambda n, *_: (0, 0, step)),
                pl.BlockSpec(
                    (2, None) + reflectors.shape[2:], lambda n, up, lo: (lo[n] // 2, step, 0, 0)
                ),
            ],
            out_specs=pl.BlockSpec(block, lambda n, *_: (0, 0, 0)),
        ),
    )(upper, lower, spread, reflectors)


def place_rows(flag, back_ref, u_ref, rows_ref, out_ref):
    @pl.when(flag == 0)
    def _():
        out_ref[...] = back_ref[...].T

    @pl.when(flag == 1)
    def _():
        out_ref[...] = rows_ref[...] - product3(split(u_ref[...]), split(back_ref[...]), NT)


def place_kernel(odd, back_ref, u_ref, work_ref, out_ref):
    panel = u_ref.shape[0]
    rows = out_ref.shape[0]
    place_rows(odd[0], back_ref, u_ref, work_ref.at[:panel], out_ref.at[:panel])
    if rows > panel:
        out_ref[panel:, :] = work_ref[panel:, :]


def place(step, back, vectors, work, odd):
    columns, panel = back.shape
    width = COLS_PER_LEAF
    rows = work.shape[0] if step == 0 else panel
    return pl.pallas_call(
        place_kernel,
        out_shape=jax.ShapeDtypeStruct(work.shape, jnp.float32),
        grid_spec=pltpu.PrefetchScalarGridSpec(
            num_scalar_prefetch=1,
            grid=(columns // width,),
            in_specs=[
                pl.BlockSpec((width, panel), lambda c, *_: (c, 0)),
                pl.BlockSpec((panel, panel), lambda c, *_: (0, 0)),
                pl.BlockSpec((rows, width), lambda c, *_: (step, c)),
            ],
            out_specs=pl.BlockSpec((rows, width), lambda c, *_: (step, c)),
        ),
        input_output_aliases={} if step == 0 else {3: 0},
    )(odd, back, vectors, work)


def pairs(row_count):
    uppers, lowers = [], []
    gap = 1
    while gap < row_count:
        for start in range(0, row_count, 2 * gap):
            uppers.append(start)
            lowers.append(start + gap)
        gap *= 2
    return jnp.array(uppers, jnp.int32), jnp.array(lowers, jnp.int32)


def spread_shards(matrix, leaf_vectors, leaf_factors, tree_vectors, tree_factors, leaf_blocks, owner):
    row_count = lax.axis_size("row")
    my_index = lax.axis_index("row")
    columns = matrix.shape[1]
    panel = tree_vectors.shape[2]
    half = panel // 2
    core = my_index % 2
    odd = ((my_index - owner) % 2).astype(jnp.int32)
    own = lax.dynamic_slice_in_dim(tree_vectors, core * half, half, axis=1)
    asked = lax.dynamic_slice_in_dim(tree_vectors, (1 - core) * half, half, axis=1)
    other = lax.ppermute(asked, "row", [(i, i ^ 1) for i in range(row_count)])
    packed = pack(own, other, tree_factors, odd)
    work, reflectors, spread = exchange(
        row_count, matrix, leaf_vectors, leaf_factors, tree_vectors, packed, leaf_blocks, odd
    )
    uppers, lowers = pairs(row_count)
    for s in range(STEPS):
        upper, lower = (uppers + owner[s]) % row_count, (lowers + owner[s]) % row_count
        done = tree(s, spread, reflectors, upper, lower)
        back = lax.all_to_all(done, "row", 0, 0).reshape(columns, panel)
        work = place(s, back, tree_vectors[s], work, odd[s : s + 1])
    return work


def plan(count):
    half = count // 2
    rows = []
    for owner in range(count):
        edges = []
        gap = 1
        while gap < count:
            for p in range(0, count, 2 * gap):
                edges.append((gap, (p + owner) % count, (p + gap + owner) % count))
            gap *= 2
        blocked = [False] * count
        inner, outer = ([], []), []
        for gap, a, b in edges:
            if a // half == b // half and not (blocked[a] or blocked[b]):
                inner[a // half].append((gap, a, b))
            else:
                outer.append((gap, a, b))
                blocked[a] = blocked[b] = True
        active = [[i for i in range(count) if blocked[i] and i // half == h] for h in (0, 1)]
        for h in (0, 1):
            where = {half * h + t: t for t in range(half)}
            row = []

            def emit(chosen, places, base):
                entries = [(0, 0, 0)] * len(places)
                used = set()
                for gap, a, b in chosen:
                    k = next(k for k, g in enumerate(places) if k not in used and g == gap)
                    used.add(k)
                    entries[k] = (where[a], where[b], b // 2)
                    where[a], where[b] = base + 2 * k, base + 2 * k + 1
                for entry in entries:
                    row.extend(entry)

            emit([e for e in inner[h] if e[0] == 1], HALF_ODD, half)
            emit([e for e in inner[h] if e[0] > 1], HALF_EVEN, half + 2 * len(HALF_ODD))
            slots = [where[i] for i in active[h]]
            row.extend(slots + [0] * (SLOTS - len(slots)))
            base = half + 2 * len(HALF_ODD) + 2 * len(HALF_EVEN)
            for side in (0, 1):
                for k, i in enumerate(active[h ^ side]):
                    where[i] = base + SLOTS * side + k
            base += 2 * SLOTS
            emit([e for e in outer if e[0] == 1], TOP_ODD, base)
            emit([e for e in outer if e[0] > 1], TOP_EVEN, base + 2 * len(TOP_ODD))
            row.extend(where[half * h + t] for t in range(half))
            rows.append(row)
    return np.array(rows, np.int32)


def tree_product(operators, index, right):
    panel, part = right.shape
    both = lax.dot_general(
        operators[index],
        jnp.concatenate(split(right), axis=1),
        NN,
        preferred_element_type=jnp.float32,
    )
    high, low = both[:panel], both[panel:]
    return high[:, :part] + (high[:, part:] + (low[:, :part] + low[:, part:]))


def pipeline_kernel(
    count, turns, lag, listed, owner, table, m_ref, y_ref, l_ref, u_ref, f_ref, tops_ref, low_ref, *scratch
):
    (
        yh, yl, yth, ytl, lth, ltl, uh, ul, uth, utl,
        wk, home, out_tops, in_tops, values, out_slots, in_slots, out_done, in_done,
        raw, mine, packs,
        odd_factors, even_factors, vectors, turned_vectors,
        raw_send, raw_recv, pack_send, pack_recv, pass_send, cross_send,
        tops_send, tops_recv, slots_send, slots_recv, done_send, done_recv,
    ) = scratch
    step_now = pl.program_id(0)
    half = count // 2
    chips = count // 2
    panel = u_ref.shape[1]
    width = m_ref.shape[1]
    part = width // 2
    block_count = m_ref.shape[0] // BLK
    listed_count = y_ref.shape[1] // BLK
    panel_blocks = panel // BLK
    me = lax.axis_index("row")
    side = me // half
    local = me % half
    chip = me // 2
    core = me % 2
    partner = me + 1 - 2 * core
    holds = (me >= half // 2) & (me < half + half // 2)
    my_step = chip % 2
    across = me + half // 2 - half * side
    primary = holds & (core == my_step)
    first_holder = half // 2 * (1 + side) + 3 * core
    row_length = table.shape[0] // (2 * count)

    def remote(source, target, send_sem, recv_sem, peer):
        return pltpu.make_async_remote_copy(
            src_ref=source,
            dst_ref=target,
            send_sem=send_sem,
            recv_sem=recv_sem,
            device_id={"row": peer},
            device_id_type=pl.DeviceIdType.MESH,
        )

    def holder(h, s, j):
        return half // 2 * (1 + h) + 2 * s + j

    def send_raw(k):
        source = (u_ref if k == 0 else f_ref).at[1 - core]
        return remote(source, raw.at[k], raw_send.at[k], raw_recv.at[k], partner)

    def send_pack():
        return remote(mine, packs.at[chip], pack_send, pack_recv.at[chip], first_holder)

    def pass_pack(c):
        return remote(packs.at[c], packs.at[c], pass_send.at[c], pack_recv.at[c], partner)

    def cross_pack(c):
        return remote(packs.at[c], packs.at[c], cross_send.at[c], pack_recv.at[c], across)

    def send_tops(t, s, j):
        return remote(
            out_tops.at[t, s, j], in_tops.at[t, local], tops_send.at[t, 2 * s + j],
            tops_recv.at[t, local], holder(side, s, j),
        )

    def receive_tops(t, source):
        return remote(
            in_tops.at[t, source], in_tops.at[t, source], tops_send.at[t, 0],
            tops_recv.at[t, source], across,
        )

    def send_slots(t):
        return remote(out_slots.at[t], in_slots.at[t], slots_send.at[t], slots_recv.at[t], across)

    def send_done(t, target):
        return remote(
            out_done.at[t, target], in_done.at[t, 2 * my_step + core], done_send.at[t, target],
            done_recv.at[t, 2 * my_step + core], half * side + target,
        )

    def receive_done(t, k):
        return remote(
            in_done.at[t, k], in_done.at[t, k], done_send.at[t, 0], done_recv.at[t, k], across
        )

    def flag(value, shape):
        return jnp.full(shape, value, jnp.int32) == 1

    def odd(s):
        return (me + count - owner[s]) % 2

    square = (panel, panel)

    @pl.when(step_now == 0)
    def _():
        barrier = pltpu.get_barrier_semaphore()
        for j in range(1, count):
            pl.semaphore_signal(
                barrier,
                inc=1,
                device_id={"row": (me + j) % count},
                device_id_type=pl.DeviceIdType.MESH,
            )
        pl.semaphore_wait(barrier, count - 1)
        for k in range(2):
            send_raw(k).start()
        for s in range(STEPS):
            yh[s], yl[s] = split(y_ref[s])
            yth[s], ytl[s] = split(y_ref[s].T)
            lth[s], ltl[s] = split(l_ref[s].T)
            uh[s], ul[s] = split(u_ref[s])
            uth[s], utl[s] = split(u_ref[s].T)
        for k in range(2):
            send_raw(k).wait_recv()
        even = 1 - jnp.where(core == 0, odd(0), odd(1))
        mine[:panel, :] = jnp.where(flag(even, square), u_ref[core], raw[0])
        own, other = f_ref[core], raw[1]
        fe = jnp.where(flag(even, square), own, other)
        fo = jnp.where(flag(even, square), other, own)
        row = lax.broadcasted_iota(jnp.int32, square, 0)
        column = lax.broadcasted_iota(jnp.int32, square, 1)
        mine[panel : 2 * panel, :] = jnp.where(row <= column, fe, fo.T)
        diagonal = jnp.sum(jnp.where(row == column, fo, 0.0), axis=0, keepdims=True)
        mine[2 * panel :, :] = jnp.broadcast_to(diagonal, (8, panel))

        @pl.when(primary)
        def _():
            packs[chip] = mine[...]

        @pl.when(jnp.logical_not(primary))
        def _():
            send_pack().start()

    def unpack(h):
        def one(q, carry):
            c = h * (chips // 2) + q
            own = c == chip

            @pl.when(jnp.logical_not(primary & own))
            def _():
                pass_pack(c).wait_recv()

            @pl.when(primary)
            def _():
                pass_pack(c).start()

            @pl.when(primary & (c // (chips // 2) == side))
            def _():
                cross_pack(c).start()

            u = packs[c, :panel, :]
            f = packs[c, panel : 2 * panel, :]
            diagonal = packs[c, 2 * panel : 2 * panel + 1, :]
            row = lax.broadcasted_iota(jnp.int32, square, 0)
            column = lax.broadcasted_iota(jnp.int32, square, 1)
            odd_factor = jnp.where(row > column, f, jnp.where(row == column, diagonal, 0.0))
            even_factor = jnp.where(row <= column, f, 0.0).T
            for ref, value in (
                (odd_factors, odd_factor), (even_factors, even_factor),
                (vectors, u), (turned_vectors, u.T),
            ):
                ref[c, :panel, :], ref[c, panel:, :] = split(value)
            return carry

        lax.fori_loop(0, chips // 2, one, 0)

    def leaf(t):
        for b in range(block_count):
            wk[b] = m_ref[b * BLK : (b + 1) * BLK, :]
        for s in range(STEPS):
            inner = range((s + 1) * panel_blocks, block_count - 1)
            numbers = range(panel_blocks, listed_count - 1)
            taken = [wk[s * panel_blocks + k] for k in range(panel_blocks)]
            taken += [wk[listed[s, k]] for k in numbers]
            taken.append(wk[block_count - 1])
            gathered = jnp.concatenate(taken, axis=0)
            projected = product3((yth[s], ytl[s]), split(gathered), NN)
            update = product3((lth[s], ltl[s]), split(projected), NN)
            change = product3((yh[s], yl[s]), split(update), NN)
            pieces = [change[k * BLK : (k + 1) * BLK] for k in range(listed_count)]
            wk[block_count - 1] -= pieces[-1]
            for block in inner:
                amount = jnp.zeros((BLK, width), jnp.float32)
                for k in numbers:
                    number = jnp.full((BLK, width), listed[s, k], jnp.int32)
                    amount = jnp.where(number == block, pieces[k], amount)
                wk[block] -= amount
            tops = [taken[k] - pieces[k] for k in range(panel_blocks)]
            tops = jnp.concatenate(tops, axis=0)
            home[t, s] = tops
            projected = product3((uth[s], utl[s]), split(tops), NN)
            tops = jnp.where(flag(odd(s), (panel, width)), projected, tops)
            for j in range(2):
                piece = tops[:, j * part : (j + 1) * part]
                out_tops[t, s, j] = piece

                @pl.when(holder(side, s, j) == me)
                def _():
                    in_tops[t, local] = piece

                @pl.when(jnp.logical_not(holds) & (t > 0))
                def _():
                    send_tops(t - 1, s, j).wait_send()

                @pl.when(holder(side, s, j) != me)
                def _():
                    send_tops(t, s, j).start()

        for b in range(STEPS * panel_blocks, block_count):
            first = (b - STEPS * panel_blocks) * BLK
            low_ref[first : first + BLK, :] = wk[b]

    start_of_row = (jnp.where(my_step == 0, owner[0], owner[1]) * 2 + side) * row_length

    def entry(k):
        return table[start_of_row + k]

    def pairs_of(first, places, base, offset, even):
        for gap in sorted(set(places)):
            group = [k for k in range(len(places)) if places[k] == gap]
            uppers = [values[entry(first + 3 * k) + offset] for k in group]
            lowers = [values[entry(first + 3 * k + 1) + offset] for k in group]
            chosen = [entry(first + 3 * k + 2) for k in group]
            if even:
                sums = [
                    a + tree_product(turned_vectors, c, b)
                    for a, b, c in zip(uppers, lowers, chosen)
                ]
                updates = [tree_product(even_factors, c, x) for c, x in zip(chosen, sums)]
                lowers = [
                    b - tree_product(vectors, c, w)
                    for b, c, w in zip(lowers, chosen, updates)
                ]
            else:
                updates = lowers = [
                    tree_product(odd_factors, c, a + b)
                    for a, b, c in zip(uppers, lowers, chosen)
                ]
            for k, a, b, w in zip(group, uppers, lowers, updates):
                values[base + offset + 2 * k] = a - w
                values[base + offset + 2 * k + 1] = b
        return first + 3 * len(places), base + 2 * len(places)

    half_entries = 3 * (len(HALF_ODD) + len(HALF_EVEN))
    slots_at = half + 2 * (len(HALF_ODD) + len(HALF_EVEN))
    top_entries = half_entries + SLOTS
    done_entries = top_entries + 3 * (len(TOP_ODD) + len(TOP_EVEN))

    def half_tree(t):
        offset = t % 2 * slots_at
        for source in range(half):

            @pl.when(source != local)
            def _():
                receive_tops(t, source).wait_recv()

            values[source + offset] = in_tops[t, source]
        first, base = pairs_of(0, HALF_ODD, half, offset, False)
        pairs_of(first, HALF_EVEN, base, offset, True)
        for k in range(SLOTS):
            out_slots[t, k] = values[entry(half_entries + k) + offset]
        send_slots(t).start()

    def top_tree(t):
        offset = t % 2 * slots_at
        for k in range(SLOTS):
            values[2 * slots_at + k] = out_slots[t, k]
        send_slots(t).wait_recv()
        for k in range(SLOTS):
            values[2 * slots_at + SLOTS + k] = in_slots[t, k]
        first, base = pairs_of(top_entries, TOP_ODD, slots_at + 2 * SLOTS, slots_at, False)
        pairs_of(first, TOP_EVEN, base, slots_at, True)
        for target in range(half):
            index = entry(done_entries + target)
            block = values[index + jnp.where(index < slots_at, offset, slots_at)]
            out_done[t, target] = block

            @pl.when(target == local)
            def _():
                in_done[t, 2 * my_step + core] = block

            @pl.when(target != local)
            def _():
                send_done(t, target).start()

    def place_tops(t):
        for s in range(STEPS):
            for j in range(2):

                @pl.when(holder(side, s, j) != me)
                def _():
                    receive_done(t, 2 * s + j).wait_recv()

            back = jnp.concatenate([in_done[t, 2 * s], in_done[t, 2 * s + 1]], axis=1)
            lower = home[t, s] - product3((uh[s], ul[s]), split(back), NN)
            tops_ref[s * panel : (s + 1) * panel, :] = jnp.where(
                flag(odd(s), (panel, width)), lower, back
            )

    @pl.when(step_now < turns)
    def _():
        leaf(step_now)

    @pl.when(step_now >= lag)
    def _():
        place_tops(step_now - lag)

    @pl.when(holds & (step_now == 1))
    def _():
        unpack(side)

    @pl.when(holds & (step_now >= 1) & (step_now < turns + 1))
    def _():
        half_tree(step_now - 1)

    @pl.when(holds & (step_now == 2))
    def _():
        unpack(1 - side)

    @pl.when(holds & (step_now >= 2) & (step_now < turns + 2))
    def _():
        top_tree(step_now - 2)

    @pl.when(step_now == turns + lag - 1)
    def _():
        for k in range(2):
            send_raw(k).wait_send()

        @pl.when(jnp.logical_not(primary))
        def _():
            send_pack().wait_send()

        @pl.when(primary)
        def _():
            for c in range(chips):
                pass_pack(c).wait_send()

                @pl.when(c // (chips // 2) == side)
                def _():
                    cross_pack(c).wait_send()

        for t in range(turns):
            for s in range(STEPS):
                for j in range(2):

                    @pl.when((holder(side, s, j) != me) & (holds | (t == turns - 1)))
                    def _():
                        send_tops(t, s, j).wait_send()

        @pl.when(holds)
        def _():
            for t in range(turns):
                send_slots(t).wait_send()
                for target in range(half):

                    @pl.when(target != local)
                    def _():
                        send_done(t, target).wait_send()


def pipeline(count, matrix, leaf_vectors, leaf_factors, tree_vectors, tree_factors, leaf_blocks, owner):
    rows, columns = matrix.shape
    width = COLS_PER_LEAF
    part = width // 2
    steps, leaf_rows, panel = leaf_vectors.shape
    turns = columns // width
    half = count // 2
    chips = count // 2
    dma = pltpu.SemaphoreType.DMA
    short = jnp.bfloat16
    top_rows = steps * panel
    lag = 4
    value_count = 2 * (half + 2 * (len(HALF_ODD) + len(HALF_EVEN)))
    value_count += 2 * (SLOTS + len(TOP_ODD) + len(TOP_EVEN))
    block = (panel, part)

    def vmem(*shape):
        return pltpu.VMEM(shape, jnp.float32)

    def whole(array):
        return pl.BlockSpec(array.shape, lambda c, *_: (0, 0, 0), pipeline_mode=pl.Buffered(1))

    tops, low = pl.pallas_call(
        functools.partial(pipeline_kernel, count, turns, lag),
        out_shape=(
            jax.ShapeDtypeStruct((top_rows, columns), jnp.float32),
            jax.ShapeDtypeStruct((rows - top_rows, columns), jnp.float32),
        ),
        grid_spec=pltpu.PrefetchScalarGridSpec(
            num_scalar_prefetch=3,
            grid=(turns + lag,),
            in_specs=[
                pl.BlockSpec((rows, width), lambda c, *_: (0, jnp.minimum(c, turns - 1))),
                whole(leaf_vectors),
                whole(leaf_factors),
                whole(tree_vectors),
                whole(tree_factors),
            ],
            out_specs=[
                pl.BlockSpec((top_rows, width), lambda c, *_: (0, jnp.maximum(c - lag, 0))),
                pl.BlockSpec((rows - top_rows, width), lambda c, *_: (0, jnp.minimum(c, turns - 1))),
            ],
            scratch_shapes=[
                *[pltpu.VMEM((steps, leaf_rows, panel), short)] * 2,
                *[pltpu.VMEM((steps, panel, leaf_rows), short)] * 2,
                *[pltpu.VMEM((steps, panel, panel), short)] * 6,
                vmem(rows // BLK, BLK, width),
                vmem(turns, steps, panel, width),
                vmem(turns, steps, 2, *block),
                vmem(turns, half, *block),
                vmem(value_count, *block),
                vmem(turns, SLOTS, *block),
                vmem(turns, SLOTS, *block),
                vmem(turns, half, *block),
                vmem(turns, 2 * steps, *block),
                vmem(2, panel, panel),
                vmem(2 * panel + 8, panel),
                vmem(chips, 2 * panel + 8, panel),
                *[pltpu.VMEM((chips, 2 * panel, panel), short)] * 4,
                dma((2,)),
                dma((2,)),
                dma,
                dma((chips,)),
                dma((chips,)),
                dma((chips,)),
                dma((turns, 2 * steps)),
                dma((turns, half)),
                dma((turns,)),
                dma((turns,)),
                dma((turns, half)),
                dma((turns, 2 * steps)),
            ],
        ),
        compiler_params=pltpu.CompilerParams(
            collective_id=0, has_side_effects=True, vmem_limit_bytes=60 * 2**20
        ),
    )(
        leaf_blocks, owner, jnp.asarray(plan(count).reshape(-1)),
        matrix, leaf_vectors, leaf_factors, tree_vectors, tree_factors,
    )
    return jnp.concatenate([tops, low], axis=0)


def shards(*arrays):
    row_count = lax.axis_size("row")
    if row_count == PLANNED_ROWS:
        return pipeline(row_count, *arrays)
    return spread_shards(*arrays)


def solution(mesh):
    return jax.shard_map(
        shards,
        mesh=mesh,
        in_specs=(
            P(("groups", "row"), None),
            P("groups", "row", None),
            P("groups", "row", None),
            P("groups", "row", None),
            P("groups", "row", None),
            P("groups", "row"),
            P("groups"),
        ),
        out_specs=P(("groups", "row"), None),
        check_vma=False,
    )
```

```python
import functools

import jax
import jax.numpy as jnp
import numpy as np
from jax import lax
from jax.experimental import pallas as pl
from jax.experimental.pallas import tpu as pltpu
from jax.sharding import PartitionSpec as P

BLK = 128
STEPS = 2
COLS_PER_LEAF = 256

PLANNED_ROWS = 16
HALF_ODD = (1, 1, 1, 1)
HALF_EVEN = (2, 2, 4)
TOP_ODD = (1, 1)
TOP_EVEN = (2, 2, 4, 4, 8)
SLOTS = 4

NN = (((1,), (0,)), ((), ()))
TN = (((0,), (0,)), ((), ()))
NT = (((1,), (1,)), ((), ()))


def split(value):
    high = value.astype(jnp.bfloat16)
    low = (value - high.astype(jnp.float32)).astype(jnp.bfloat16)
    return high, low


def product3(left, right, dims):
    def one(a, b):
        return lax.dot_general(a, b, dims, preferred_element_type=jnp.float32)

    return one(left[0], right[0]) + (one(left[0], right[1]) + one(left[1], right[0]))


def corner_masks(half):
    row = lax.broadcasted_iota(jnp.int32, (half, half), 0)
    column = lax.broadcasted_iota(jnp.int32, (half, half), 1)
    return row < column, row == column


def pack_kernel(odd, own_ref, other_ref, f_ref, all_ref):
    half = own_ref.shape[1]
    above, on = corner_masks(half)
    for s in range(STEPS):
        out_ref = all_ref.at[s]
        out_ref[:half, :] = own_ref[s]

        @pl.when(odd[s] == 1)
        def _():
            out_ref[:half, :] = other_ref[s]

        first = f_ref[s, :half, :half]
        second = f_ref[s, half:, half:]
        out_ref[half : 2 * half, :half] = jnp.where(above | on, first, second.T)
        out_ref[half : 2 * half, half:] = f_ref[s, :half, half:]
        diagonal = jnp.sum(jnp.where(on, second, 0.0), axis=0, keepdims=True)
        line = jnp.concatenate([diagonal, jnp.zeros_like(diagonal)], axis=1)
        out_ref[2 * half :, :] = jnp.broadcast_to(line, (8, 2 * half))


def pack(own, other, factors, odd):
    steps, half, panel = own.shape
    shape = (steps, panel + 8, panel)
    return pl.pallas_call(
        pack_kernel,
        out_shape=jax.ShapeDtypeStruct(shape, jnp.float32),
        grid_spec=pltpu.PrefetchScalarGridSpec(
            num_scalar_prefetch=1,
            grid=(1,),
            in_specs=[
                pl.BlockSpec(own.shape, lambda c, *_: (0, 0, 0)),
                pl.BlockSpec(other.shape, lambda c, *_: (0, 0, 0)),
                pl.BlockSpec(factors.shape, lambda c, *_: (0, 0, 0)),
            ],
            out_specs=pl.BlockSpec(shape, lambda c, *_: (0, 0, 0)),
        ),
    )(odd, own, other, factors)


def chip_at(place, chips):
    return jnp.where(place < chips // 2, 2 * place, 2 * (chips - 1 - place) + 1)


def place_of(chip, chips):
    return jnp.where(chip % 2 == 0, chip // 2, chips - 1 - chip // 2)


def leaf_block(listed, odd, m_ref, u_ref, out_ref, tops_ref, first, parts):
    yh, yl, yth, ytl, lth, ltl, uh, ul = parts
    panel = u_ref.shape[1]
    width = out_ref.shape[1]
    block_count = out_ref.shape[0] // BLK
    listed_count = yh.shape[1] // BLK
    panel_blocks = panel // BLK
    out_ref[...] = m_ref[...]
    for s in range(STEPS):
        inner = range((s + 1) * panel_blocks, block_count - 1)
        numbers = {
            k: jnp.full((BLK, width), listed[s, k], jnp.int32)
            for k in range(panel_blocks, listed_count - 1)
        }
        taken = [out_ref[s * panel : (s + 1) * panel, :]]
        for number in numbers.values():
            block_rows = jnp.zeros((BLK, width), jnp.float32)
            for block in inner:
                here = out_ref[block * BLK : (block + 1) * BLK, :]
                block_rows = jnp.where(number == block, here, block_rows)
            taken.append(block_rows)
        taken.append(out_ref[(block_count - 1) * BLK :, :])
        gathered = jnp.concatenate(taken, axis=0)
        projected = product3((yth[s], ytl[s]), split(gathered), NN)
        update = product3((lth[s], ltl[s]), split(projected), NN)
        change = product3((yh[s], yl[s]), split(update), NN)
        pieces = [change[k * BLK : (k + 1) * BLK] for k in range(listed_count)]
        fixed = [(s * panel_blocks + k, pieces[k]) for k in range(panel_blocks)]
        for block, piece in fixed + [(block_count - 1, pieces[-1])]:
            out_ref[block * BLK : (block + 1) * BLK, :] -= piece
        for block in inner:
            amount = jnp.zeros((BLK, width), jnp.float32)
            for k, number in numbers.items():
                amount = jnp.where(number == block, pieces[k], amount)
            out_ref[block * BLK : (block + 1) * BLK, :] -= amount
    for s in range(STEPS):
        turned = out_ref[s * panel : (s + 1) * panel, :].T
        projected = product3(split(turned), (uh[s], ul[s]), NN)
        flag = jnp.full(turned.shape, odd[s], jnp.int32)
        tops_ref[pl.ds(first, width), s * panel : (s + 1) * panel] = jnp.where(
            flag == 1, projected, turned
        )


def exchange_kernel(count, listed, odd, m_ref, y_ref, l_ref, u_ref, p_ref, work_ref, g_ref, r_ref, *rest):
    parts = rest[:8]
    t_ref, ring_send, ring_recv, pass_send, pass_recv, a2a_send, a2a_recv, own_sem = rest[8:]
    turn = pl.program_id(0)
    turns = t_ref.shape[0] // m_ref.shape[1]
    me = lax.axis_index("row")
    chips = count // 2
    share = t_ref.shape[0] // count
    core = me % 2
    place = place_of(me // 2, chips)

    def device(offset):
        return chip_at((place + offset + chips) % chips, chips) * 2 + core

    partner = me + 1 - 2 * core
    right, left = device(1), device(-1)

    def remote(source, target, send_sem, recv_sem, peer):
        return pltpu.make_async_remote_copy(
            src_ref=source,
            dst_ref=target,
            send_sem=send_sem,
            recv_sem=recv_sem,
            device_id={"row": peer},
            device_id_type=pl.DeviceIdType.MESH,
        )

    lengths = {(0, 0): chips // 2, (0, 1): chips - 1 - chips // 2}
    lengths[1, 1], lengths[1, 0] = lengths[0, 0], lengths[0, 1]
    longest = max(lengths.values())

    def hop(s, way, t):
        origin = device(-t if way == 0 else t)
        source = p_ref.at[s] if t == 0 else g_ref.at[origin, s]
        return remote(
            source,
            g_ref.at[origin, s],
            ring_send.at[s, way, t],
            ring_recv.at[s, way, t],
            right if way == 0 else left,
        )

    def hand(s, way, t):
        if t < 0:
            return remote(
                p_ref.at[s], g_ref.at[me, s], pass_send.at[s, 0], pass_recv.at[s, 0], partner
            )
        origin = device(-t - 1 if way == 0 else t + 1)
        slot = 1 + (t if way == 0 else lengths[s, 0] + t)
        piece = g_ref.at[origin, s]
        return remote(piece, piece, pass_send.at[s, slot], pass_recv.at[s, slot], partner)

    def columns_of(peer):
        return t_ref.at[pl.ds(pl.multiple_of(peer * share, 8), share), :]

    def scatter(j):
        peer = (me + j) % count
        return remote(columns_of(peer), r_ref.at[me], a2a_send.at[j - 1], a2a_recv.at[j - 1], peer)

    def keep(s):
        return pltpu.make_async_copy(p_ref.at[s], g_ref.at[me, s], own_sem.at[s])

    def keep_columns():
        return pltpu.make_async_copy(columns_of(me), r_ref.at[me], own_sem.at[STEPS])

    def advance(t):
        for s, way in lengths:
            if t < lengths[s, way]:
                hop(s, way, t).wait_recv()
                if t + 1 < lengths[s, way]:
                    hop(s, way, t + 1).start()
                hand(s, way, t).start()

    @pl.when(turn == 0)
    def _():
        barrier = pltpu.get_barrier_semaphore()
        for j in range(1, count):
            pl.semaphore_signal(
                barrier,
                inc=1,
                device_id={"row": (me + j) % count},
                device_id_type=pl.DeviceIdType.MESH,
            )
        pl.semaphore_wait(barrier, count - 1)
        for s, way in lengths:
            if lengths[s, way] > 0:
                hop(s, way, 0).start()
        for s in range(STEPS):
            hand(s, 0, -1).start()
            keep(s).start()
        yh, yl, yth, ytl, lth, ltl, uh, ul = parts
        for s in range(STEPS):
            yh[s], yl[s] = split(y_ref[s])
            yth[s], ytl[s] = split(y_ref[s].T)
            lth[s], ltl[s] = split(l_ref[s].T)
            uh[s], ul[s] = split(u_ref[s])

    first = pl.multiple_of(turn * m_ref.shape[1], m_ref.shape[1])
    leaf_block(listed, odd, m_ref, u_ref, work_ref, t_ref, first, parts)

    early = min(turns - 1, longest)
    for t in range(early):

        @pl.when(turn == t)
        def _():
            advance(t)

    @pl.when(turn == turns - 1)
    def _():
        todo = [(j + count // 2 - 1) % (count - 1) + 1 for j in range(count - 1)]
        rounds = max(longest - early, 1)
        size = -(-len(todo) // rounds)
        keep_columns().start()
        for t in range(rounds):
            for j in todo[t * size : (t + 1) * size]:
                scatter(j).start()
            advance(early + t)
        for s, way in lengths:
            for t in range(lengths[s, way]):
                hop(s, way, t).wait_send()
                hand(s, way, t).wait()
        for s in range(STEPS):
            hand(s, 0, -1).wait()
            keep(s).wait()
        keep_columns().wait()
        for j in todo:
            scatter(j).wait()


def exchange(count, matrix, leaf_vectors, leaf_factors, tree_vectors, packed, leaf_blocks, odd):
    rows, columns = matrix.shape
    width = COLS_PER_LEAF
    steps, leaf_rows, panel = leaf_vectors.shape
    chips = count // 2
    dma = pltpu.SemaphoreType.DMA
    half_type = jnp.bfloat16

    def whole(array):
        return pl.BlockSpec(array.shape, lambda c, *_: (0, 0, 0))

    return pl.pallas_call(
        functools.partial(exchange_kernel, count),
        out_shape=(
            jax.ShapeDtypeStruct((rows, columns), jnp.float32),
            jax.ShapeDtypeStruct((count,) + packed.shape, jnp.float32),
            jax.ShapeDtypeStruct((count, columns // count, steps * panel), jnp.float32),
        ),
        grid_spec=pltpu.PrefetchScalarGridSpec(
            num_scalar_prefetch=2,
            grid=(columns // width,),
            in_specs=[
                pl.BlockSpec((rows, width), lambda c, *_: (0, c)),
                whole(leaf_vectors),
                whole(leaf_factors),
                whole(tree_vectors),
                whole(packed),
            ],
            out_specs=[
                pl.BlockSpec((rows, width), lambda c, *_: (0, c)),
                pl.BlockSpec(memory_space=pl.ANY),
                pl.BlockSpec(memory_space=pl.ANY),
            ],
            scratch_shapes=[
                *[pltpu.VMEM((steps, leaf_rows, panel), half_type)] * 2,
                *[pltpu.VMEM((steps, panel, leaf_rows), half_type)] * 2,
                *[pltpu.VMEM((steps, panel, panel), half_type)] * 4,
                pltpu.VMEM((columns, steps * panel), jnp.float32),
                dma((steps, 2, chips)),
                dma((steps, 2, chips)),
                dma((steps, chips)),
                dma((steps, chips)),
                dma((count - 1,)),
                dma((count - 1,)),
                dma((steps + 1,)),
            ],
        ),
        compiler_params=pltpu.CompilerParams(collective_id=0, has_side_effects=True),
    )(leaf_blocks, odd, matrix, leaf_vectors, leaf_factors, tree_vectors, packed)


def tree_kernel(upper, lower, x_ref, g_ref, out_ref):
    node = pl.program_id(0)
    panel = g_ref.shape[2]
    half = panel // 2
    first_level = x_ref.shape[0] // 2

    @pl.when(node == 0)
    def _():
        out_ref[...] = x_ref[...]

    a, b = upper[node], lower[node]
    slot = lax.rem(b, 2)
    above, on = corner_masks(half)
    corner = g_ref[slot, half : 2 * half, :half]
    diagonal = g_ref[slot, 2 * half : 2 * half + 1, :half]
    top = jnp.concatenate(
        [jnp.where(above | on, corner, 0.0), g_ref[slot, half : 2 * half, half:]], axis=1
    )
    last = jnp.where(above, corner.T, jnp.where(on, diagonal, 0.0))
    bottom = jnp.concatenate([jnp.zeros_like(last), last], axis=1)
    f = split(jnp.concatenate([top, bottom], axis=0))
    xa, xb = out_ref[a], out_ref[b]

    @pl.when(node < first_level)
    def _():
        w = product3(split(xa + xb), f, NN)
        out_ref[a] = xa - w
        out_ref[b] = w

    @pl.when(node >= first_level)
    def _():
        u = split(jnp.concatenate([g_ref[0, :half, :], g_ref[1, :half, :]], axis=0))
        w = product3(split(xa + product3(split(xb), u, NN)), f, NN)
        out_ref[a] = xa - w
        out_ref[b] = xb - product3(split(w), u, NT)


def tree(step, spread, reflectors, upper, lower):
    devices, width, both = spread.shape
    block = (devices, width, both // STEPS)
    return pl.pallas_call(
        tree_kernel,
        out_shape=jax.ShapeDtypeStruct(block, jnp.float32),
        grid_spec=pltpu.PrefetchScalarGridSpec(
            num_scalar_prefetch=2,
            grid=(devices - 1,),
            in_specs=[
                pl.BlockSpec(block, lambda n, *_: (0, 0, step)),
                pl.BlockSpec(
                    (2, None) + reflectors.shape[2:], lambda n, up, lo: (lo[n] // 2, step, 0, 0)
                ),
            ],
            out_specs=pl.BlockSpec(block, lambda n, *_: (0, 0, 0)),
        ),
    )(upper, lower, spread, reflectors)


def place_rows(flag, back_ref, u_ref, rows_ref, out_ref):
    @pl.when(flag == 0)
    def _():
        out_ref[...] = back_ref[...].T

    @pl.when(flag == 1)
    def _():
        out_ref[...] = rows_ref[...] - product3(split(u_ref[...]), split(back_ref[...]), NT)


def place_kernel(odd, back_ref, u_ref, work_ref, out_ref):
    panel = u_ref.shape[0]
    rows = out_ref.shape[0]
    place_rows(odd[0], back_ref, u_ref, work_ref.at[:panel], out_ref.at[:panel])
    if rows > panel:
        out_ref[panel:, :] = work_ref[panel:, :]


def place(step, back, vectors, work, odd):
    columns, panel = back.shape
    width = COLS_PER_LEAF
    rows = work.shape[0] if step == 0 else panel
    return pl.pallas_call(
        place_kernel,
        out_shape=jax.ShapeDtypeStruct(work.shape, jnp.float32),
        grid_spec=pltpu.PrefetchScalarGridSpec(
            num_scalar_prefetch=1,
            grid=(columns // width,),
            in_specs=[
                pl.BlockSpec((width, panel), lambda c, *_: (c, 0)),
                pl.BlockSpec((panel, panel), lambda c, *_: (0, 0)),
                pl.BlockSpec((rows, width), lambda c, *_: (step, c)),
            ],
            out_specs=pl.BlockSpec((rows, width), lambda c, *_: (step, c)),
        ),
        input_output_aliases={} if step == 0 else {3: 0},
    )(odd, back, vectors, work)


def pairs(row_count):
    uppers, lowers = [], []
    gap = 1
    while gap < row_count:
        for start in range(0, row_count, 2 * gap):
            uppers.append(start)
            lowers.append(start + gap)
        gap *= 2
    return jnp.array(uppers, jnp.int32), jnp.array(lowers, jnp.int32)


def spread_shards(matrix, leaf_vectors, leaf_factors, tree_vectors, tree_factors, leaf_blocks, owner):
    row_count = lax.axis_size("row")
    my_index = lax.axis_index("row")
    columns = matrix.shape[1]
    panel = tree_vectors.shape[2]
    half = panel // 2
    core = my_index % 2
    odd = ((my_index - owner) % 2).astype(jnp.int32)
    own = lax.dynamic_slice_in_dim(tree_vectors, core * half, half, axis=1)
    asked = lax.dynamic_slice_in_dim(tree_vectors, (1 - core) * half, half, axis=1)
    other = lax.ppermute(asked, "row", [(i, i ^ 1) for i in range(row_count)])
    packed = pack(own, other, tree_factors, odd)
    work, reflectors, spread = exchange(
        row_count, matrix, leaf_vectors, leaf_factors, tree_vectors, packed, leaf_blocks, odd
    )
    uppers, lowers = pairs(row_count)
    for s in range(STEPS):
        upper, lower = (uppers + owner[s]) % row_count, (lowers + owner[s]) % row_count
        done = tree(s, spread, reflectors, upper, lower)
        back = lax.all_to_all(done, "row", 0, 0).reshape(columns, panel)
        work = place(s, back, tree_vectors[s], work, odd[s : s + 1])
    return work


def plan(count):
    half = count // 2
    rows = []
    for owner in range(count):
        edges = []
        gap = 1
        while gap < count:
            for p in range(0, count, 2 * gap):
                edges.append((gap, (p + owner) % count, (p + gap + owner) % count))
            gap *= 2
        blocked = [False] * count
        inner, outer = ([], []), []
        for gap, a, b in edges:
            if a // half == b // half and not (blocked[a] or blocked[b]):
                inner[a // half].append((gap, a, b))
            else:
                outer.append((gap, a, b))
                blocked[a] = blocked[b] = True
        active = [[i for i in range(count) if blocked[i] and i // half == h] for h in (0, 1)]
        for h in (0, 1):
            where = {half * h + t: t for t in range(half)}
            row = []

            def emit(chosen, places, base):
                entries = [(0, 0, 0)] * len(places)
                used = set()
                for gap, a, b in chosen:
                    k = next(k for k, g in enumerate(places) if k not in used and g == gap)
                    used.add(k)
                    entries[k] = (where[a], where[b], b // 2)
                    where[a], where[b] = base + 2 * k, base + 2 * k + 1
                for entry in entries:
                    row.extend(entry)

            emit([e for e in inner[h] if e[0] == 1], HALF_ODD, half)
            emit([e for e in inner[h] if e[0] > 1], HALF_EVEN, half + 2 * len(HALF_ODD))
            slots = [where[i] for i in active[h]]
            row.extend(slots + [0] * (SLOTS - len(slots)))
            base = half + 2 * len(HALF_ODD) + 2 * len(HALF_EVEN)
            for side in (0, 1):
                for k, i in enumerate(active[h ^ side]):
                    where[i] = base + SLOTS * side + k
            base += 2 * SLOTS
            emit([e for e in outer if e[0] == 1], TOP_ODD, base)
            emit([e for e in outer if e[0] > 1], TOP_EVEN, base + 2 * len(TOP_ODD))
            row.extend(where[half * h + t] for t in range(half))
            rows.append(row)
    return np.array(rows, np.int32)


def tree_product(operators, index, right):
    panel, part = right.shape
    both = lax.dot_general(
        operators[index],
        jnp.concatenate(split(right), axis=1),
        NN,
        preferred_element_type=jnp.float32,
    )
    high, low = both[:panel], both[panel:]
    return high[:, :part] + (high[:, part:] + (low[:, :part] + low[:, part:]))


def pipeline_kernel(
    count, turns, lag, listed, owner, table, m_ref, y_ref, l_ref, u_ref, f_ref, tops_ref, low_ref, *scratch
):
    (
        yh, yl, yth, ytl, lth, ltl, uh, ul, uth, utl,
        wk, home, out_tops, in_tops, values, out_slots, in_slots, out_done, in_done,
        raw, mine, packs, lent,
        odd_factors, even_factors, vectors, turned_vectors,
        raw_send, raw_recv, pack_send, pack_recv, pass_send, cross_send, far_send,
        tops_send, tops_recv, lent_send, lent_recv, slots_send, slots_recv, done_send, done_recv,
    ) = scratch
    step_now = pl.program_id(0)
    half = count // 2
    chips = count // 2
    panel = u_ref.shape[1]
    width = m_ref.shape[1]
    part = width // 2
    block_count = m_ref.shape[0] // BLK
    listed_count = y_ref.shape[1] // BLK
    panel_blocks = panel // BLK
    me = lax.axis_index("row")
    side = me // half
    local = me % half
    chip = me // 2
    core = me % 2
    partner = me + 1 - 2 * core
    holds = (me >= half // 2) & (me < half + half // 2)
    my_step = chip % 2
    beside = me + 2 - 4 * my_step
    across = me + half // 2 - half * side
    primary = holds & (core == my_step)
    first_holder = half // 2 * (1 + side) + 3 * core
    far_holder = half // 2 * (2 - side) + 3 * core
    row_length = table.shape[0] // (2 * count)

    def remote(source, target, send_sem, recv_sem, peer):
        return pltpu.make_async_remote_copy(
            src_ref=source,
            dst_ref=target,
            send_sem=send_sem,
            recv_sem=recv_sem,
            device_id={"row": peer},
            device_id_type=pl.DeviceIdType.MESH,
        )

    def holder(h, s, j):
        return half // 2 * (1 + h) + 2 * s + j

    def send_raw(k):
        source = (u_ref if k == 0 else f_ref).at[1 - core]
        return remote(source, raw.at[k], raw_send.at[k], raw_recv.at[k], partner)

    def send_pack():
        return remote(mine, packs.at[chip], pack_send, pack_recv.at[chip], first_holder)

    def pass_pack(c):
        return remote(packs.at[c], packs.at[c], pass_send.at[c], pack_recv.at[c], partner)

    def cross_pack(c):
        return remote(packs.at[c], packs.at[c], cross_send.at[c], pack_recv.at[c], across)

    def send_far():
        return remote(mine, packs.at[chip], far_send, pack_recv.at[chip], far_holder)

    def send_tops(t, s, j):
        return remote(
            out_tops.at[t, s, j], in_tops.at[t, local], tops_send.at[t, 2 * s + j],
            tops_recv.at[t, local], holder(side, s, j),
        )

    def lend_tops(t, j):
        s = 1 - my_step
        return remote(
            out_tops.at[t, s, j], lent.at[t, j], tops_send.at[t, 2 * s + j],
            lent_recv.at[t, j], beside,
        )

    def pass_tops(t, j):
        return remote(
            lent.at[t, j], in_tops.at[t, beside % half], lent_send.at[t, j],
            tops_recv.at[t, beside % half], holder(side, my_step, j),
        )

    def receive_tops(t, source):
        return remote(
            in_tops.at[t, source], in_tops.at[t, source], tops_send.at[t, 0],
            tops_recv.at[t, source], across,
        )

    def send_slots(t):
        return remote(out_slots.at[t], in_slots.at[t], slots_send.at[t], slots_recv.at[t], across)

    def send_done(t, target):
        return remote(
            out_done.at[t, target], in_done.at[t, 2 * my_step + core], done_send.at[t, target],
            done_recv.at[t, 2 * my_step + core], half * side + target,
        )

    def receive_done(t, k):
        return remote(
            in_done.at[t, k], in_done.at[t, k], done_send.at[t, 0], done_recv.at[t, k], across
        )

    def flag(value, shape):
        return jnp.full(shape, value, jnp.int32) == 1

    def odd(s):
        return (me + count - owner[s]) % 2

    square = (panel, panel)

    @pl.when(step_now == 0)
    def _():
        barrier = pltpu.get_barrier_semaphore()
        for j in range(1, count):
            pl.semaphore_signal(
                barrier,
                inc=1,
                device_id={"row": (me + j) % count},
                device_id_type=pl.DeviceIdType.MESH,
            )
        pl.semaphore_wait(barrier, count - 1)
        for k in range(2):
            send_raw(k).start()
        for s in range(STEPS):
            uh[s], ul[s] = split(u_ref[s])
            uth[s], utl[s] = split(u_ref[s].T)
        for k in range(2):
            send_raw(k).wait_recv()
        even = 1 - jnp.where(core == 0, odd(0), odd(1))
        mine[:panel, :] = jnp.where(flag(even, square), u_ref[core], raw[0])
        own, other = f_ref[core], raw[1]
        fe = jnp.where(flag(even, square), own, other)
        fo = jnp.where(flag(even, square), other, own)
        row = lax.broadcasted_iota(jnp.int32, square, 0)
        column = lax.broadcasted_iota(jnp.int32, square, 1)
        mine[panel : 2 * panel, :] = jnp.where(row <= column, fe, fo.T)
        diagonal = jnp.sum(jnp.where(row == column, fo, 0.0), axis=0, keepdims=True)
        mine[2 * panel :, :] = jnp.broadcast_to(diagonal, (8, panel))

        @pl.when(primary)
        def _():
            packs[chip] = mine[...]

        @pl.when(jnp.logical_not(primary))
        def _():
            send_pack().start()

        @pl.when(holds)
        def _():
            send_far().start()

        for s in range(STEPS):
            yh[s], yl[s] = split(y_ref[s])
            yth[s], ytl[s] = split(y_ref[s].T)
            lth[s], ltl[s] = split(l_ref[s].T)

    def hand_on(h):
        near = chips // 4 * (1 - h)
        for q in range(chips // 2):
            c = h * (chips // 2) + (near + q) % (chips // 2)

            @pl.when(c != chip)
            def _():
                pass_pack(c).wait_recv()

            pass_pack(c).start()
            if q >= chips // 4:

                @pl.when(h == side)
                def _():
                    cross_pack(c).start()

    def unpack(h):
        def one(q, carry):
            c = h * (chips // 2) + q

            @pl.when(jnp.logical_not(primary))
            def _():
                pass_pack(c).wait_recv()

            u = packs[c, :panel, :]
            f = packs[c, panel : 2 * panel, :]
            diagonal = packs[c, 2 * panel : 2 * panel + 1, :]
            row = lax.broadcasted_iota(jnp.int32, square, 0)
            column = lax.broadcasted_iota(jnp.int32, square, 1)
            odd_factor = jnp.where(row > column, f, jnp.where(row == column, diagonal, 0.0))
            even_factor = jnp.where(row <= column, f, 0.0).T
            for ref, value in (
                (odd_factors, odd_factor), (even_factors, even_factor),
                (vectors, u), (turned_vectors, u.T),
            ):
                ref[c, :panel, :], ref[c, panel:, :] = split(value)
            return carry

        lax.fori_loop(0, chips // 2, one, 0)

    def leaf(t):
        for b in range(block_count):
            wk[b] = m_ref[b * BLK : (b + 1) * BLK, :]
        for s in range(STEPS):
            inner = range((s + 1) * panel_blocks, block_count - 1)
            numbers = range(panel_blocks, listed_count - 1)
            taken = [wk[s * panel_blocks + k] for k in range(panel_blocks)]
            taken += [wk[listed[s, k]] for k in numbers]
            taken.append(wk[block_count - 1])
            gathered = jnp.concatenate(taken, axis=0)
            projected = product3((yth[s], ytl[s]), split(gathered), NN)
            update = product3((lth[s], ltl[s]), split(projected), NN)
            change = product3((yh[s], yl[s]), split(update), NN)
            pieces = [change[k * BLK : (k + 1) * BLK] for k in range(listed_count)]
            wk[block_count - 1] -= pieces[-1]
            for block in inner:
                amount = jnp.zeros((BLK, width), jnp.float32)
                for k in numbers:
                    number = jnp.full((BLK, width), listed[s, k], jnp.int32)
                    amount = jnp.where(number == block, pieces[k], amount)
                wk[block] -= amount
            tops = [taken[k] - pieces[k] for k in range(panel_blocks)]
            tops = jnp.concatenate(tops, axis=0)
            home[t, s] = tops
            projected = product3((uth[s], utl[s]), split(tops), NN)
            tops = jnp.where(flag(odd(s), (panel, width)), projected, tops)
            for j in range(2):
                piece = tops[:, j * part : (j + 1) * part]
                out_tops[t, s, j] = piece

                @pl.when(holder(side, s, j) == me)
                def _():
                    in_tops[t, local] = piece

        @pl.when(holds)
        def _():
            for j in range(2):
                for s in range(STEPS):

                    @pl.when(holder(side, s, j) != me)
                    def _():
                        send_tops(t, s, j).start()

        @pl.when(jnp.logical_not(holds))
        def _():
            for j in range(2):
                lend_tops(t, j).start()

            @pl.when(t == 0)
            def _():
                send_pack().wait_send()

            @pl.when(t > 0)
            def _():
                send_tops(t - 1, my_step, 1).wait_send()

            send_tops(t, my_step, 0).start()
            lend_tops(t, 0).wait_recv()

            @pl.when(t > 0)
            def _():
                pass_tops(t - 1, 1).wait_send()

            pass_tops(t, 0).start()
            send_tops(t, my_step, 0).wait_send()
            send_tops(t, my_step, 1).start()
            lend_tops(t, 1).wait_recv()
            pass_tops(t, 0).wait_send()
            pass_tops(t, 1).start()

        for b in range(STEPS * panel_blocks, block_count):
            first = (b - STEPS * panel_blocks) * BLK
            low_ref[first : first + BLK, :] = wk[b]

    start_of_row = (jnp.where(my_step == 0, owner[0], owner[1]) * 2 + side) * row_length

    def entry(k):
        return table[start_of_row + k]

    def pairs_of(first, places, base, offset, even):
        for gap in sorted(set(places)):
            group = [k for k in range(len(places)) if places[k] == gap]
            uppers = [values[entry(first + 3 * k) + offset] for k in group]
            lowers = [values[entry(first + 3 * k + 1) + offset] for k in group]
            chosen = [entry(first + 3 * k + 2) for k in group]
            if even:
                sums = [
                    a + tree_product(turned_vectors, c, b)
                    for a, b, c in zip(uppers, lowers, chosen)
                ]
                updates = [tree_product(even_factors, c, x) for c, x in zip(chosen, sums)]
                lowers = [
                    b - tree_product(vectors, c, w)
                    for b, c, w in zip(lowers, chosen, updates)
                ]
            else:
                updates = lowers = [
                    tree_product(odd_factors, c, a + b)
                    for a, b, c in zip(uppers, lowers, chosen)
                ]
            for k, a, b, w in zip(group, uppers, lowers, updates):
                values[base + offset + 2 * k] = a - w
                values[base + offset + 2 * k + 1] = b
        return first + 3 * len(places), base + 2 * len(places)

    half_entries = 3 * (len(HALF_ODD) + len(HALF_EVEN))
    slots_at = half + 2 * (len(HALF_ODD) + len(HALF_EVEN))
    top_entries = half_entries + SLOTS
    done_entries = top_entries + 3 * (len(TOP_ODD) + len(TOP_EVEN))

    def half_tree(t):
        offset = t % 2 * slots_at
        for source in range(half):

            @pl.when(source != local)
            def _():
                receive_tops(t, source).wait_recv()

            values[source + offset] = in_tops[t, source]
        first, base = pairs_of(0, HALF_ODD, half, offset, False)
        pairs_of(first, HALF_EVEN, base, offset, True)
        for k in range(SLOTS):
            out_slots[t, k] = values[entry(half_entries + k) + offset]
        send_slots(t).start()

    def top_tree(t):
        offset = t % 2 * slots_at
        for k in range(SLOTS):
            values[2 * slots_at + k] = out_slots[t, k]
        send_slots(t).wait_recv()
        for k in range(SLOTS):
            values[2 * slots_at + SLOTS + k] = in_slots[t, k]
        first, base = pairs_of(top_entries, TOP_ODD, slots_at + 2 * SLOTS, slots_at, False)
        pairs_of(first, TOP_EVEN, base, slots_at, True)
        for k in range(half):
            target = k + side * (half - 1 - 2 * k)
            index = entry(done_entries + target)
            block = values[index + jnp.where(index < slots_at, offset, slots_at)]
            out_done[t, target] = block

            @pl.when(target == local)
            def _():
                in_done[t, 2 * my_step + core] = block

            @pl.when(target != local)
            def _():
                send_done(t, target).start()

    def place_tops(t):
        for s in range(STEPS):
            for j in range(2):

                @pl.when(holder(side, s, j) != me)
                def _():
                    receive_done(t, 2 * s + j).wait_recv()

            back = jnp.concatenate([in_done[t, 2 * s], in_done[t, 2 * s + 1]], axis=1)
            lower = home[t, s] - product3((uh[s], ul[s]), split(back), NN)
            tops_ref[s * panel : (s + 1) * panel, :] = jnp.where(
                flag(odd(s), (panel, width)), lower, back
            )

    @pl.when(primary & (step_now == 0))
    def _():
        hand_on(side)

    @pl.when(step_now < turns)
    def _():
        leaf(step_now)

    @pl.when(holds & (step_now == 1))
    def _():
        unpack(side)

    @pl.when(holds & (step_now >= 1) & (step_now < turns + 1))
    def _():
        half_tree(step_now - 1)

    @pl.when(primary & (step_now == 2))
    def _():
        hand_on(1 - side)

    @pl.when(holds & (step_now == 2))
    def _():
        unpack(1 - side)

    @pl.when(holds & (step_now >= 2) & (step_now < turns + 2))
    def _():
        top_tree(step_now - 2)

    @pl.when(step_now >= lag)
    def _():
        place_tops(step_now - lag)

    @pl.when(step_now == turns + lag - 1)
    def _():
        for k in range(2):
            send_raw(k).wait_send()

        @pl.when(holds & jnp.logical_not(primary))
        def _():
            send_pack().wait_send()

        @pl.when(primary)
        def _():
            for c in range(chips):
                pass_pack(c).wait_send()
            for q in range(chips // 4):
                cross_pack(side * 3 * (chips // 4) + q).wait_send()

        @pl.when(holds)
        def _():
            send_far().wait_send()

        @pl.when(jnp.logical_not(holds))
        def _():
            for t in range(turns):
                for j in range(2):
                    lend_tops(t, j).wait_send()
            send_tops(turns - 1, my_step, 1).wait_send()
            pass_tops(turns - 1, 1).wait_send()

        @pl.when(holds)
        def _():
            for t in range(turns):
                for s in range(STEPS):
                    for j in range(2):

                        @pl.when(holder(side, s, j) != me)
                        def _():
                            send_tops(t, s, j).wait_send()

                send_slots(t).wait_send()
                for target in range(half):

                    @pl.when(target != local)
                    def _():
                        send_done(t, target).wait_send()


def pipeline(count, matrix, leaf_vectors, leaf_factors, tree_vectors, tree_factors, leaf_blocks, owner):
    rows, columns = matrix.shape
    width = COLS_PER_LEAF
    part = width // 2
    steps, leaf_rows, panel = leaf_vectors.shape
    turns = columns // width
    half = count // 2
    chips = count // 2
    dma = pltpu.SemaphoreType.DMA
    short = jnp.bfloat16
    top_rows = steps * panel
    lag = 4
    value_count = 2 * (half + 2 * (len(HALF_ODD) + len(HALF_EVEN)))
    value_count += 2 * (SLOTS + len(TOP_ODD) + len(TOP_EVEN))
    block = (panel, part)

    def vmem(*shape):
        return pltpu.VMEM(shape, jnp.float32)

    def whole(array):
        return pl.BlockSpec(array.shape, lambda c, *_: (0, 0, 0), pipeline_mode=pl.Buffered(1))

    tops, low = pl.pallas_call(
        functools.partial(pipeline_kernel, count, turns, lag),
        out_shape=(
            jax.ShapeDtypeStruct((top_rows, columns), jnp.float32),
            jax.ShapeDtypeStruct((rows - top_rows, columns), jnp.float32),
        ),
        grid_spec=pltpu.PrefetchScalarGridSpec(
            num_scalar_prefetch=3,
            grid=(turns + lag,),
            in_specs=[
                pl.BlockSpec((rows, width), lambda c, *_: (0, jnp.minimum(c, turns - 1))),
                whole(leaf_vectors),
                whole(leaf_factors),
                whole(tree_vectors),
                whole(tree_factors),
            ],
            out_specs=[
                pl.BlockSpec((top_rows, width), lambda c, *_: (0, jnp.maximum(c - lag, 0))),
                pl.BlockSpec((rows - top_rows, width), lambda c, *_: (0, jnp.minimum(c, turns - 1))),
            ],
            scratch_shapes=[
                *[pltpu.VMEM((steps, leaf_rows, panel), short)] * 2,
                *[pltpu.VMEM((steps, panel, leaf_rows), short)] * 2,
                *[pltpu.VMEM((steps, panel, panel), short)] * 6,
                vmem(rows // BLK, BLK, width),
                vmem(turns, steps, panel, width),
                vmem(turns, steps, 2, *block),
                vmem(turns, half, *block),
                vmem(value_count, *block),
                vmem(turns, SLOTS, *block),
                vmem(turns, SLOTS, *block),
                vmem(turns, half, *block),
                vmem(turns, 2 * steps, *block),
                vmem(2, panel, panel),
                vmem(2 * panel + 8, panel),
                vmem(chips, 2 * panel + 8, panel),
                vmem(turns, 2, *block),
                *[pltpu.VMEM((chips, 2 * panel, panel), short)] * 4,
                dma((2,)),
                dma((2,)),
                dma,
                dma((chips,)),
                dma((chips,)),
                dma((chips,)),
                dma,
                dma((turns, 2 * steps)),
                dma((turns, half)),
                dma((turns, 2)),
                dma((turns, 2)),
                dma((turns,)),
                dma((turns,)),
                dma((turns, half)),
                dma((turns, 2 * steps)),
            ],
        ),
        compiler_params=pltpu.CompilerParams(
            collective_id=0, has_side_effects=True, vmem_limit_bytes=60 * 2**20
        ),
    )(
        leaf_blocks, owner, jnp.asarray(plan(count).reshape(-1)),
        matrix, leaf_vectors, leaf_factors, tree_vectors, tree_factors,
    )
    return jnp.concatenate([tops, low], axis=0)


def shards(*arrays):
    row_count = lax.axis_size("row")
    if row_count == PLANNED_ROWS:
        return pipeline(row_count, *arrays)
    return spread_shards(*arrays)


def solution(mesh):
    return jax.shard_map(
        shards,
        mesh=mesh,
        in_specs=(
            P(("groups", "row"), None),
            P("groups", "row", None),
            P("groups", "row", None),
            P("groups", "row", None),
            P("groups", "row", None),
            P("groups", "row"),
            P("groups"),
        ),
        out_specs=P(("groups", "row"), None),
        check_vma=False,
    )
```

```python
import functools

import jax
import jax.numpy as jnp
import numpy as np
from jax import lax
from jax.experimental import pallas as pl
from jax.experimental.pallas import tpu as pltpu
from jax.sharding import PartitionSpec as P

BLK = 128
STEPS = 2
COLS_PER_LEAF = 256

PLANNED_ROWS = 16
HALF_ODD = (1, 1, 1, 1)
HALF_EVEN = (2, 2, 4)
TOP_ODD = (1, 1)
TOP_EVEN = (2, 2, 4, 4, 8)
SLOTS = 4

NN = (((1,), (0,)), ((), ()))
TN = (((0,), (0,)), ((), ()))
NT = (((1,), (1,)), ((), ()))


def split(value):
    high = value.astype(jnp.bfloat16)
    low = (value - high.astype(jnp.float32)).astype(jnp.bfloat16)
    return high, low


def product3(left, right, dims):
    def one(a, b):
        return lax.dot_general(a, b, dims, preferred_element_type=jnp.float32)

    return one(left[0], right[0]) + (one(left[0], right[1]) + one(left[1], right[0]))


def corner_masks(half):
    row = lax.broadcasted_iota(jnp.int32, (half, half), 0)
    column = lax.broadcasted_iota(jnp.int32, (half, half), 1)
    return row < column, row == column


def pack_kernel(odd, own_ref, other_ref, f_ref, all_ref):
    half = own_ref.shape[1]
    above, on = corner_masks(half)
    for s in range(STEPS):
        out_ref = all_ref.at[s]
        out_ref[:half, :] = own_ref[s]

        @pl.when(odd[s] == 1)
        def _():
            out_ref[:half, :] = other_ref[s]

        first = f_ref[s, :half, :half]
        second = f_ref[s, half:, half:]
        out_ref[half : 2 * half, :half] = jnp.where(above | on, first, second.T)
        out_ref[half : 2 * half, half:] = f_ref[s, :half, half:]
        diagonal = jnp.sum(jnp.where(on, second, 0.0), axis=0, keepdims=True)
        line = jnp.concatenate([diagonal, jnp.zeros_like(diagonal)], axis=1)
        out_ref[2 * half :, :] = jnp.broadcast_to(line, (8, 2 * half))


def pack(own, other, factors, odd):
    steps, half, panel = own.shape
    shape = (steps, panel + 8, panel)
    return pl.pallas_call(
        pack_kernel,
        out_shape=jax.ShapeDtypeStruct(shape, jnp.float32),
        grid_spec=pltpu.PrefetchScalarGridSpec(
            num_scalar_prefetch=1,
            grid=(1,),
            in_specs=[
                pl.BlockSpec(own.shape, lambda c, *_: (0, 0, 0)),
                pl.BlockSpec(other.shape, lambda c, *_: (0, 0, 0)),
                pl.BlockSpec(factors.shape, lambda c, *_: (0, 0, 0)),
            ],
            out_specs=pl.BlockSpec(shape, lambda c, *_: (0, 0, 0)),
        ),
    )(odd, own, other, factors)


def chip_at(place, chips):
    return jnp.where(place < chips // 2, 2 * place, 2 * (chips - 1 - place) + 1)


def place_of(chip, chips):
    return jnp.where(chip % 2 == 0, chip // 2, chips - 1 - chip // 2)


def leaf_block(listed, odd, m_ref, u_ref, out_ref, tops_ref, first, parts):
    yh, yl, yth, ytl, lth, ltl, uh, ul = parts
    panel = u_ref.shape[1]
    width = out_ref.shape[1]
    block_count = out_ref.shape[0] // BLK
    listed_count = yh.shape[1] // BLK
    panel_blocks = panel // BLK
    out_ref[...] = m_ref[...]
    for s in range(STEPS):
        inner = range((s + 1) * panel_blocks, block_count - 1)
        numbers = {
            k: jnp.full((BLK, width), listed[s, k], jnp.int32)
            for k in range(panel_blocks, listed_count - 1)
        }
        taken = [out_ref[s * panel : (s + 1) * panel, :]]
        for number in numbers.values():
            block_rows = jnp.zeros((BLK, width), jnp.float32)
            for block in inner:
                here = out_ref[block * BLK : (block + 1) * BLK, :]
                block_rows = jnp.where(number == block, here, block_rows)
            taken.append(block_rows)
        taken.append(out_ref[(block_count - 1) * BLK :, :])
        gathered = jnp.concatenate(taken, axis=0)
        projected = product3((yth[s], ytl[s]), split(gathered), NN)
        update = product3((lth[s], ltl[s]), split(projected), NN)
        change = product3((yh[s], yl[s]), split(update), NN)
        pieces = [change[k * BLK : (k + 1) * BLK] for k in range(listed_count)]
        fixed = [(s * panel_blocks + k, pieces[k]) for k in range(panel_blocks)]
        for block, piece in fixed + [(block_count - 1, pieces[-1])]:
            out_ref[block * BLK : (block + 1) * BLK, :] -= piece
        for block in inner:
            amount = jnp.zeros((BLK, width), jnp.float32)
            for k, number in numbers.items():
                amount = jnp.where(number == block, pieces[k], amount)
            out_ref[block * BLK : (block + 1) * BLK, :] -= amount
    for s in range(STEPS):
        turned = out_ref[s * panel : (s + 1) * panel, :].T
        projected = product3(split(turned), (uh[s], ul[s]), NN)
        flag = jnp.full(turned.shape, odd[s], jnp.int32)
        tops_ref[pl.ds(first, width), s * panel : (s + 1) * panel] = jnp.where(
            flag == 1, projected, turned
        )


def exchange_kernel(count, listed, odd, m_ref, y_ref, l_ref, u_ref, p_ref, work_ref, g_ref, r_ref, *rest):
    parts = rest[:8]
    t_ref, ring_send, ring_recv, pass_send, pass_recv, a2a_send, a2a_recv, own_sem = rest[8:]
    turn = pl.program_id(0)
    turns = t_ref.shape[0] // m_ref.shape[1]
    me = lax.axis_index("row")
    chips = count // 2
    share = t_ref.shape[0] // count
    core = me % 2
    place = place_of(me // 2, chips)

    def device(offset):
        return chip_at((place + offset + chips) % chips, chips) * 2 + core

    partner = me + 1 - 2 * core
    right, left = device(1), device(-1)

    def remote(source, target, send_sem, recv_sem, peer):
        return pltpu.make_async_remote_copy(
            src_ref=source,
            dst_ref=target,
            send_sem=send_sem,
            recv_sem=recv_sem,
            device_id={"row": peer},
            device_id_type=pl.DeviceIdType.MESH,
        )

    lengths = {(0, 0): chips // 2, (0, 1): chips - 1 - chips // 2}
    lengths[1, 1], lengths[1, 0] = lengths[0, 0], lengths[0, 1]
    longest = max(lengths.values())

    def hop(s, way, t):
        origin = device(-t if way == 0 else t)
        source = p_ref.at[s] if t == 0 else g_ref.at[origin, s]
        return remote(
            source,
            g_ref.at[origin, s],
            ring_send.at[s, way, t],
            ring_recv.at[s, way, t],
            right if way == 0 else left,
        )

    def hand(s, way, t):
        if t < 0:
            return remote(
                p_ref.at[s], g_ref.at[me, s], pass_send.at[s, 0], pass_recv.at[s, 0], partner
            )
        origin = device(-t - 1 if way == 0 else t + 1)
        slot = 1 + (t if way == 0 else lengths[s, 0] + t)
        piece = g_ref.at[origin, s]
        return remote(piece, piece, pass_send.at[s, slot], pass_recv.at[s, slot], partner)

    def columns_of(peer):
        return t_ref.at[pl.ds(pl.multiple_of(peer * share, 8), share), :]

    def scatter(j):
        peer = (me + j) % count
        return remote(columns_of(peer), r_ref.at[me], a2a_send.at[j - 1], a2a_recv.at[j - 1], peer)

    def keep(s):
        return pltpu.make_async_copy(p_ref.at[s], g_ref.at[me, s], own_sem.at[s])

    def keep_columns():
        return pltpu.make_async_copy(columns_of(me), r_ref.at[me], own_sem.at[STEPS])

    def advance(t):
        for s, way in lengths:
            if t < lengths[s, way]:
                hop(s, way, t).wait_recv()
                if t + 1 < lengths[s, way]:
                    hop(s, way, t + 1).start()
                hand(s, way, t).start()

    @pl.when(turn == 0)
    def _():
        barrier = pltpu.get_barrier_semaphore()
        for j in range(1, count):
            pl.semaphore_signal(
                barrier,
                inc=1,
                device_id={"row": (me + j) % count},
                device_id_type=pl.DeviceIdType.MESH,
            )
        pl.semaphore_wait(barrier, count - 1)
        for s, way in lengths:
            if lengths[s, way] > 0:
                hop(s, way, 0).start()
        for s in range(STEPS):
            hand(s, 0, -1).start()
            keep(s).start()
        yh, yl, yth, ytl, lth, ltl, uh, ul = parts
        for s in range(STEPS):
            yh[s], yl[s] = split(y_ref[s])
            yth[s], ytl[s] = split(y_ref[s].T)
            lth[s], ltl[s] = split(l_ref[s].T)
            uh[s], ul[s] = split(u_ref[s])

    first = pl.multiple_of(turn * m_ref.shape[1], m_ref.shape[1])
    leaf_block(listed, odd, m_ref, u_ref, work_ref, t_ref, first, parts)

    early = min(turns - 1, longest)
    for t in range(early):

        @pl.when(turn == t)
        def _():
            advance(t)

    @pl.when(turn == turns - 1)
    def _():
        todo = [(j + count // 2 - 1) % (count - 1) + 1 for j in range(count - 1)]
        rounds = max(longest - early, 1)
        size = -(-len(todo) // rounds)
        keep_columns().start()
        for t in range(rounds):
            for j in todo[t * size : (t + 1) * size]:
                scatter(j).start()
            advance(early + t)
        for s, way in lengths:
            for t in range(lengths[s, way]):
                hop(s, way, t).wait_send()
                hand(s, way, t).wait()
        for s in range(STEPS):
            hand(s, 0, -1).wait()
            keep(s).wait()
        keep_columns().wait()
        for j in todo:
            scatter(j).wait()


def exchange(count, matrix, leaf_vectors, leaf_factors, tree_vectors, packed, leaf_blocks, odd):
    rows, columns = matrix.shape
    width = COLS_PER_LEAF
    steps, leaf_rows, panel = leaf_vectors.shape
    chips = count // 2
    dma = pltpu.SemaphoreType.DMA
    half_type = jnp.bfloat16

    def whole(array):
        return pl.BlockSpec(array.shape, lambda c, *_: (0, 0, 0))

    return pl.pallas_call(
        functools.partial(exchange_kernel, count),
        out_shape=(
            jax.ShapeDtypeStruct((rows, columns), jnp.float32),
            jax.ShapeDtypeStruct((count,) + packed.shape, jnp.float32),
            jax.ShapeDtypeStruct((count, columns // count, steps * panel), jnp.float32),
        ),
        grid_spec=pltpu.PrefetchScalarGridSpec(
            num_scalar_prefetch=2,
            grid=(columns // width,),
            in_specs=[
                pl.BlockSpec((rows, width), lambda c, *_: (0, c)),
                whole(leaf_vectors),
                whole(leaf_factors),
                whole(tree_vectors),
                whole(packed),
            ],
            out_specs=[
                pl.BlockSpec((rows, width), lambda c, *_: (0, c)),
                pl.BlockSpec(memory_space=pl.ANY),
                pl.BlockSpec(memory_space=pl.ANY),
            ],
            scratch_shapes=[
                *[pltpu.VMEM((steps, leaf_rows, panel), half_type)] * 2,
                *[pltpu.VMEM((steps, panel, leaf_rows), half_type)] * 2,
                *[pltpu.VMEM((steps, panel, panel), half_type)] * 4,
                pltpu.VMEM((columns, steps * panel), jnp.float32),
                dma((steps, 2, chips)),
                dma((steps, 2, chips)),
                dma((steps, chips)),
                dma((steps, chips)),
                dma((count - 1,)),
                dma((count - 1,)),
                dma((steps + 1,)),
            ],
        ),
        compiler_params=pltpu.CompilerParams(collective_id=0, has_side_effects=True),
    )(leaf_blocks, odd, matrix, leaf_vectors, leaf_factors, tree_vectors, packed)


def tree_kernel(upper, lower, x_ref, g_ref, out_ref):
    node = pl.program_id(0)
    panel = g_ref.shape[2]
    half = panel // 2
    first_level = x_ref.shape[0] // 2

    @pl.when(node == 0)
    def _():
        out_ref[...] = x_ref[...]

    a, b = upper[node], lower[node]
    slot = lax.rem(b, 2)
    above, on = corner_masks(half)
    corner = g_ref[slot, half : 2 * half, :half]
    diagonal = g_ref[slot, 2 * half : 2 * half + 1, :half]
    top = jnp.concatenate(
        [jnp.where(above | on, corner, 0.0), g_ref[slot, half : 2 * half, half:]], axis=1
    )
    last = jnp.where(above, corner.T, jnp.where(on, diagonal, 0.0))
    bottom = jnp.concatenate([jnp.zeros_like(last), last], axis=1)
    f = split(jnp.concatenate([top, bottom], axis=0))
    xa, xb = out_ref[a], out_ref[b]

    @pl.when(node < first_level)
    def _():
        w = product3(split(xa + xb), f, NN)
        out_ref[a] = xa - w
        out_ref[b] = w

    @pl.when(node >= first_level)
    def _():
        u = split(jnp.concatenate([g_ref[0, :half, :], g_ref[1, :half, :]], axis=0))
        w = product3(split(xa + product3(split(xb), u, NN)), f, NN)
        out_ref[a] = xa - w
        out_ref[b] = xb - product3(split(w), u, NT)


def tree(step, spread, reflectors, upper, lower):
    devices, width, both = spread.shape
    block = (devices, width, both // STEPS)
    return pl.pallas_call(
        tree_kernel,
        out_shape=jax.ShapeDtypeStruct(block, jnp.float32),
        grid_spec=pltpu.PrefetchScalarGridSpec(
            num_scalar_prefetch=2,
            grid=(devices - 1,),
            in_specs=[
                pl.BlockSpec(block, lambda n, *_: (0, 0, step)),
                pl.BlockSpec(
                    (2, None) + reflectors.shape[2:], lambda n, up, lo: (lo[n] // 2, step, 0, 0)
                ),
            ],
            out_specs=pl.BlockSpec(block, lambda n, *_: (0, 0, 0)),
        ),
    )(upper, lower, spread, reflectors)


def place_rows(flag, back_ref, u_ref, rows_ref, out_ref):
    @pl.when(flag == 0)
    def _():
        out_ref[...] = back_ref[...].T

    @pl.when(flag == 1)
    def _():
        out_ref[...] = rows_ref[...] - product3(split(u_ref[...]), split(back_ref[...]), NT)


def place_kernel(odd, back_ref, u_ref, work_ref, out_ref):
    panel = u_ref.shape[0]
    rows = out_ref.shape[0]
    place_rows(odd[0], back_ref, u_ref, work_ref.at[:panel], out_ref.at[:panel])
    if rows > panel:
        out_ref[panel:, :] = work_ref[panel:, :]


def place(step, back, vectors, work, odd):
    columns, panel = back.shape
    width = COLS_PER_LEAF
    rows = work.shape[0] if step == 0 else panel
    return pl.pallas_call(
        place_kernel,
        out_shape=jax.ShapeDtypeStruct(work.shape, jnp.float32),
        grid_spec=pltpu.PrefetchScalarGridSpec(
            num_scalar_prefetch=1,
            grid=(columns // width,),
            in_specs=[
                pl.BlockSpec((width, panel), lambda c, *_: (c, 0)),
                pl.BlockSpec((panel, panel), lambda c, *_: (0, 0)),
                pl.BlockSpec((rows, width), lambda c, *_: (step, c)),
            ],
            out_specs=pl.BlockSpec((rows, width), lambda c, *_: (step, c)),
        ),
        input_output_aliases={} if step == 0 else {3: 0},
    )(odd, back, vectors, work)


def pairs(row_count):
    uppers, lowers = [], []
    gap = 1
    while gap < row_count:
        for start in range(0, row_count, 2 * gap):
            uppers.append(start)
            lowers.append(start + gap)
        gap *= 2
    return jnp.array(uppers, jnp.int32), jnp.array(lowers, jnp.int32)


def spread_shards(matrix, leaf_vectors, leaf_factors, tree_vectors, tree_factors, leaf_blocks, owner):
    row_count = lax.axis_size("row")
    my_index = lax.axis_index("row")
    columns = matrix.shape[1]
    panel = tree_vectors.shape[2]
    half = panel // 2
    core = my_index % 2
    odd = ((my_index - owner) % 2).astype(jnp.int32)
    own = lax.dynamic_slice_in_dim(tree_vectors, core * half, half, axis=1)
    asked = lax.dynamic_slice_in_dim(tree_vectors, (1 - core) * half, half, axis=1)
    other = lax.ppermute(asked, "row", [(i, i ^ 1) for i in range(row_count)])
    packed = pack(own, other, tree_factors, odd)
    work, reflectors, spread = exchange(
        row_count, matrix, leaf_vectors, leaf_factors, tree_vectors, packed, leaf_blocks, odd
    )
    uppers, lowers = pairs(row_count)
    for s in range(STEPS):
        upper, lower = (uppers + owner[s]) % row_count, (lowers + owner[s]) % row_count
        done = tree(s, spread, reflectors, upper, lower)
        back = lax.all_to_all(done, "row", 0, 0).reshape(columns, panel)
        work = place(s, back, tree_vectors[s], work, odd[s : s + 1])
    return work


def plan(count):
    half = count // 2
    rows = []
    for owner in range(count):
        edges = []
        gap = 1
        while gap < count:
            for p in range(0, count, 2 * gap):
                edges.append((gap, (p + owner) % count, (p + gap + owner) % count))
            gap *= 2
        blocked = [False] * count
        inner, outer = ([], []), []
        for gap, a, b in edges:
            if a // half == b // half and not (blocked[a] or blocked[b]):
                inner[a // half].append((gap, a, b))
            else:
                outer.append((gap, a, b))
                blocked[a] = blocked[b] = True
        active = [[i for i in range(count) if blocked[i] and i // half == h] for h in (0, 1)]
        for h in (0, 1):
            where = {half * h + t: t for t in range(half)}
            row = []

            def emit(chosen, places, base):
                entries = [(0, 0, 0)] * len(places)
                used = set()
                for gap, a, b in chosen:
                    k = next(k for k, g in enumerate(places) if k not in used and g == gap)
                    used.add(k)
                    entries[k] = (where[a], where[b], b // 2)
                    where[a], where[b] = base + 2 * k, base + 2 * k + 1
                for entry in entries:
                    row.extend(entry)

            emit([e for e in inner[h] if e[0] == 1], HALF_ODD, half)
            emit([e for e in inner[h] if e[0] > 1], HALF_EVEN, half + 2 * len(HALF_ODD))
            slots = [where[i] for i in active[h]]
            row.extend(slots + [0] * (SLOTS - len(slots)))
            base = half + 2 * len(HALF_ODD) + 2 * len(HALF_EVEN)
            for side in (0, 1):
                for k, i in enumerate(active[h ^ side]):
                    where[i] = base + SLOTS * side + k
            base += 2 * SLOTS
            emit([e for e in outer if e[0] == 1], TOP_ODD, base)
            emit([e for e in outer if e[0] > 1], TOP_EVEN, base + 2 * len(TOP_ODD))
            row.extend(where[half * h + t] for t in range(half))
            rows.append(row)
    return np.array(rows, np.int32)


def tree_product(operators, index, right):
    panel, part = right.shape
    high, low = split(right)
    both = lax.dot_general(
        operators[index, :panel],
        jnp.concatenate([high, low], axis=1),
        NN,
        preferred_element_type=jnp.float32,
    )
    rest = lax.dot_general(
        operators[index, panel:], high, NN, preferred_element_type=jnp.float32
    )
    return both[:, :part] + (both[:, part:] + rest)


def pipeline_kernel(
    count, turns, lag, listed, owner, table, m_ref, y_ref, l_ref, u_ref, f_ref, tops_ref, low_ref, *scratch
):
    (
        yh, yl, yth, ytl, lth, ltl, uh, ul, uth, utl,
        wk, home, out_tops, in_tops, values, out_slots, in_slots, out_done, in_done,
        raw, mine, packs, lent,
        odd_factors, even_factors, vectors, turned_vectors,
        raw_send, raw_recv, pack_send, pack_recv, pass_send, cross_send, far_send,
        tops_send, tops_recv, lent_send, lent_recv, slots_send, slots_recv, done_send, done_recv,
    ) = scratch
    step_now = pl.program_id(0)
    half = count // 2
    chips = count // 2
    panel = u_ref.shape[1]
    width = m_ref.shape[1]
    part = width // 2
    block_count = m_ref.shape[0] // BLK
    listed_count = y_ref.shape[1] // BLK
    panel_blocks = panel // BLK
    me = lax.axis_index("row")
    side = me // half
    local = me % half
    chip = me // 2
    core = me % 2
    partner = me + 1 - 2 * core
    holds = (me >= half // 2) & (me < half + half // 2)
    my_step = chip % 2
    beside = me + 2 - 4 * my_step
    across = me + half // 2 - half * side
    primary = holds & (core == my_step)
    first_holder = half // 2 * (1 + side) + 3 * core
    far_holder = half // 2 * (2 - side) + 3 * core
    row_length = table.shape[0] // (2 * count)

    def remote(source, target, send_sem, recv_sem, peer):
        return pltpu.make_async_remote_copy(
            src_ref=source,
            dst_ref=target,
            send_sem=send_sem,
            recv_sem=recv_sem,
            device_id={"row": peer},
            device_id_type=pl.DeviceIdType.MESH,
        )

    def holder(h, s, j):
        return half // 2 * (1 + h) + 2 * s + j

    def send_raw(k):
        source = (u_ref if k == 0 else f_ref).at[1 - core]
        return remote(source, raw.at[k], raw_send.at[k], raw_recv.at[k], partner)

    def send_pack():
        return remote(mine, packs.at[chip], pack_send, pack_recv.at[chip], first_holder)

    def pass_pack(c):
        return remote(packs.at[c], packs.at[c], pass_send.at[c], pack_recv.at[c], partner)

    def cross_pack(c):
        return remote(packs.at[c], packs.at[c], cross_send.at[c], pack_recv.at[c], across)

    def send_far():
        return remote(mine, packs.at[chip], far_send, pack_recv.at[chip], far_holder)

    def send_tops(t, s, j):
        return remote(
            out_tops.at[t, s, j], in_tops.at[t, local], tops_send.at[t, 2 * s + j],
            tops_recv.at[t, local], holder(side, s, j),
        )

    def lend_tops(t, j):
        s = 1 - my_step
        return remote(
            out_tops.at[t, s, j], lent.at[t, j], tops_send.at[t, 2 * s + j],
            lent_recv.at[t, j], beside,
        )

    def pass_tops(t, j):
        return remote(
            lent.at[t, j], in_tops.at[t, beside % half], lent_send.at[t, j],
            tops_recv.at[t, beside % half], holder(side, my_step, j),
        )

    def receive_tops(t, source):
        return remote(
            in_tops.at[t, source], in_tops.at[t, source], tops_send.at[t, 0],
            tops_recv.at[t, source], across,
        )

    def send_slots(t):
        return remote(out_slots.at[t], in_slots.at[t], slots_send.at[t], slots_recv.at[t], across)

    def send_done(t, target):
        return remote(
            out_done.at[t, target], in_done.at[t, 2 * my_step + core], done_send.at[t, target],
            done_recv.at[t, 2 * my_step + core], half * side + target,
        )

    def receive_done(t, k):
        return remote(
            in_done.at[t, k], in_done.at[t, k], done_send.at[t, 0], done_recv.at[t, k], across
        )

    def flag(value, shape):
        return jnp.full(shape, value, jnp.int32) == 1

    def odd(s):
        return (me + count - owner[s]) % 2

    square = (panel, panel)

    @pl.when(step_now == 0)
    def _():
        barrier = pltpu.get_barrier_semaphore()
        for j in range(1, count):
            pl.semaphore_signal(
                barrier,
                inc=1,
                device_id={"row": (me + j) % count},
                device_id_type=pl.DeviceIdType.MESH,
            )
        pl.semaphore_wait(barrier, count - 1)
        for k in range(2):
            send_raw(k).start()
        for s in range(STEPS):
            uh[s], ul[s] = split(u_ref[s])
            uth[s], utl[s] = split(u_ref[s].T)
        for k in range(2):
            send_raw(k).wait_recv()
        even = 1 - jnp.where(core == 0, odd(0), odd(1))
        mine[:panel, :] = jnp.where(flag(even, square), u_ref[core], raw[0])
        own, other = f_ref[core], raw[1]
        fe = jnp.where(flag(even, square), own, other)
        fo = jnp.where(flag(even, square), other, own)
        row = lax.broadcasted_iota(jnp.int32, square, 0)
        column = lax.broadcasted_iota(jnp.int32, square, 1)
        mine[panel : 2 * panel, :] = jnp.where(row <= column, fe, fo.T)
        diagonal = jnp.sum(jnp.where(row == column, fo, 0.0), axis=0, keepdims=True)
        mine[2 * panel :, :] = jnp.broadcast_to(diagonal, (8, panel))

        @pl.when(primary)
        def _():
            packs[chip] = mine[...]

        @pl.when(jnp.logical_not(primary))
        def _():
            send_pack().start()

        @pl.when(holds)
        def _():
            send_far().start()

        for s in range(STEPS):
            yh[s], yl[s] = split(y_ref[s])
            yth[s], ytl[s] = split(y_ref[s].T)
            lth[s], ltl[s] = split(l_ref[s].T)

    def hand_on(h):
        near = chips // 4 * (1 - h)
        for q in range(chips // 2):
            c = h * (chips // 2) + (near + q) % (chips // 2)

            @pl.when(c != chip)
            def _():
                pass_pack(c).wait_recv()

            pass_pack(c).start()
            if q >= chips // 4:

                @pl.when(h == side)
                def _():
                    cross_pack(c).start()

    def unpack(h):
        def one(q, carry):
            c = h * (chips // 2) + q

            @pl.when(jnp.logical_not(primary))
            def _():
                pass_pack(c).wait_recv()

            u = packs[c, :panel, :]
            f = packs[c, panel : 2 * panel, :]
            diagonal = packs[c, 2 * panel : 2 * panel + 1, :]
            row = lax.broadcasted_iota(jnp.int32, square, 0)
            column = lax.broadcasted_iota(jnp.int32, square, 1)
            odd_factor = jnp.where(row > column, f, jnp.where(row == column, diagonal, 0.0))
            even_factor = jnp.where(row <= column, f, 0.0).T
            for ref, value in (
                (odd_factors, odd_factor), (even_factors, even_factor),
                (vectors, u), (turned_vectors, u.T),
            ):
                ref[c, :panel, :], ref[c, panel:, :] = split(value)
            return carry

        lax.fori_loop(0, chips // 2, one, 0)

    def leaf(t):
        for b in range(block_count):
            wk[b] = m_ref[b * BLK : (b + 1) * BLK, :]
        for s in range(STEPS):
            inner = range((s + 1) * panel_blocks, block_count - 1)
            numbers = range(panel_blocks, listed_count - 1)
            taken = [wk[s * panel_blocks + k] for k in range(panel_blocks)]
            taken += [wk[listed[s, k]] for k in numbers]
            taken.append(wk[block_count - 1])
            gathered = jnp.concatenate(taken, axis=0)
            projected = product3((yth[s], ytl[s]), split(gathered), NN)
            update = product3((lth[s], ltl[s]), split(projected), NN)
            change = product3((yh[s], yl[s]), split(update), NN)
            pieces = [change[k * BLK : (k + 1) * BLK] for k in range(listed_count)]
            wk[block_count - 1] -= pieces[-1]
            for block in inner:
                amount = jnp.zeros((BLK, width), jnp.float32)
                for k in numbers:
                    number = jnp.full((BLK, width), listed[s, k], jnp.int32)
                    amount = jnp.where(number == block, pieces[k], amount)
                wk[block] -= amount
            tops = [taken[k] - pieces[k] for k in range(panel_blocks)]
            tops = jnp.concatenate(tops, axis=0)
            home[t, s] = tops
            projected = product3((uth[s], utl[s]), split(tops), NN)
            tops = jnp.where(flag(odd(s), (panel, width)), projected, tops)
            for j in range(2):
                piece = tops[:, j * part : (j + 1) * part]
                out_tops[t, s, j] = piece

                @pl.when(holder(side, s, j) == me)
                def _():
                    in_tops[t, local] = piece

        @pl.when(holds)
        def _():
            for j in range(2):
                for s in range(STEPS):

                    @pl.when(holder(side, s, j) != me)
                    def _():
                        send_tops(t, s, j).start()

        @pl.when(jnp.logical_not(holds))
        def _():
            for j in range(2):
                lend_tops(t, j).start()

            @pl.when(t == 0)
            def _():
                send_pack().wait_send()

            for j in range(2):
                send_tops(t, my_step, j).start()
            for j in range(2):
                lend_tops(t, j).wait_recv()
                pass_tops(t, j).start()

        for b in range(STEPS * panel_blocks, block_count):
            first = (b - STEPS * panel_blocks) * BLK
            low_ref[first : first + BLK, :] = wk[b]

    start_of_row = (jnp.where(my_step == 0, owner[0], owner[1]) * 2 + side) * row_length

    def entry(k):
        return table[start_of_row + k]

    def pairs_of(first, places, base, offset, even):
        for gap in sorted(set(places)):
            group = [k for k in range(len(places)) if places[k] == gap]
            uppers = [values[entry(first + 3 * k) + offset] for k in group]
            lowers = [values[entry(first + 3 * k + 1) + offset] for k in group]
            chosen = [entry(first + 3 * k + 2) for k in group]
            if even:
                sums = [
                    a + tree_product(turned_vectors, c, b)
                    for a, b, c in zip(uppers, lowers, chosen)
                ]
                updates = [tree_product(even_factors, c, x) for c, x in zip(chosen, sums)]
                lowers = [
                    b - tree_product(vectors, c, w)
                    for b, c, w in zip(lowers, chosen, updates)
                ]
            else:
                updates = lowers = [
                    tree_product(odd_factors, c, a + b)
                    for a, b, c in zip(uppers, lowers, chosen)
                ]
            for k, a, b, w in zip(group, uppers, lowers, updates):
                values[base + offset + 2 * k] = a - w
                values[base + offset + 2 * k + 1] = b
        return first + 3 * len(places), base + 2 * len(places)

    half_entries = 3 * (len(HALF_ODD) + len(HALF_EVEN))
    slots_at = half + 2 * (len(HALF_ODD) + len(HALF_EVEN))
    top_entries = half_entries + SLOTS
    done_entries = top_entries + 3 * (len(TOP_ODD) + len(TOP_EVEN))

    def half_tree(t):
        offset = t % 2 * slots_at
        for source in range(half):

            @pl.when(source != local)
            def _():
                receive_tops(t, source).wait_recv()

            values[source + offset] = in_tops[t, source]
        first, base = pairs_of(0, HALF_ODD, half, offset, False)
        pairs_of(first, HALF_EVEN, base, offset, True)
        for k in range(SLOTS):
            out_slots[t, k] = values[entry(half_entries + k) + offset]
        send_slots(t).start()

    def top_tree(t):
        offset = t % 2 * slots_at
        for k in range(SLOTS):
            values[2 * slots_at + k] = out_slots[t, k]
        send_slots(t).wait_recv()
        for k in range(SLOTS):
            values[2 * slots_at + SLOTS + k] = in_slots[t, k]
        first, base = pairs_of(top_entries, TOP_ODD, slots_at + 2 * SLOTS, slots_at, False)
        pairs_of(first, TOP_EVEN, base, slots_at, True)
        for k in range(half):
            target = k + side * (half - 1 - 2 * k)
            index = entry(done_entries + target)
            block = values[index + jnp.where(index < slots_at, offset, slots_at)]
            out_done[t, target] = block

            @pl.when(target == local)
            def _():
                in_done[t, 2 * my_step + core] = block

            @pl.when(target != local)
            def _():
                send_done(t, target).start()

    def place_tops(t):
        for s in range(STEPS):
            for j in range(2):

                @pl.when(holder(side, s, j) != me)
                def _():
                    receive_done(t, 2 * s + j).wait_recv()

            back = jnp.concatenate([in_done[t, 2 * s], in_done[t, 2 * s + 1]], axis=1)
            lower = home[t, s] - product3((uh[s], ul[s]), split(back), NN)
            tops_ref[s * panel : (s + 1) * panel, :] = jnp.where(
                flag(odd(s), (panel, width)), lower, back
            )

    @pl.when(primary & (step_now == 0))
    def _():
        hand_on(side)

    @pl.when(step_now < turns)
    def _():
        leaf(step_now)

    @pl.when(holds & (step_now == 1))
    def _():
        unpack(side)

    @pl.when(holds & (step_now >= 1) & (step_now < turns + 1))
    def _():
        half_tree(step_now - 1)

    @pl.when(primary & (step_now == 2))
    def _():
        hand_on(1 - side)

    @pl.when(holds & (step_now == 2))
    def _():
        unpack(1 - side)

    @pl.when(holds & (step_now >= 2) & (step_now < turns + 2))
    def _():
        top_tree(step_now - 2)

    @pl.when(step_now >= lag)
    def _():
        place_tops(step_now - lag)

    @pl.when(step_now == turns + lag - 1)
    def _():
        for k in range(2):
            send_raw(k).wait_send()

        @pl.when(holds & jnp.logical_not(primary))
        def _():
            send_pack().wait_send()

        @pl.when(primary)
        def _():
            for c in range(chips):
                pass_pack(c).wait_send()
            for q in range(chips // 4):
                cross_pack(side * 3 * (chips // 4) + q).wait_send()

        @pl.when(holds)
        def _():
            send_far().wait_send()

        @pl.when(jnp.logical_not(holds))
        def _():
            for t in range(turns):
                for j in range(2):
                    lend_tops(t, j).wait_send()
                    send_tops(t, my_step, j).wait_send()
                    pass_tops(t, j).wait_send()

        @pl.when(holds)
        def _():
            for t in range(turns):
                for s in range(STEPS):
                    for j in range(2):

                        @pl.when(holder(side, s, j) != me)
                        def _():
                            send_tops(t, s, j).wait_send()

                send_slots(t).wait_send()
                for target in range(half):

                    @pl.when(target != local)
                    def _():
                        send_done(t, target).wait_send()


def pipeline(count, matrix, leaf_vectors, leaf_factors, tree_vectors, tree_factors, leaf_blocks, owner):
    rows, columns = matrix.shape
    width = COLS_PER_LEAF
    part = width // 2
    steps, leaf_rows, panel = leaf_vectors.shape
    turns = columns // width
    half = count // 2
    chips = count // 2
    dma = pltpu.SemaphoreType.DMA
    short = jnp.bfloat16
    top_rows = steps * panel
    lag = 4
    value_count = 2 * (half + 2 * (len(HALF_ODD) + len(HALF_EVEN)))
    value_count += 2 * (SLOTS + len(TOP_ODD) + len(TOP_EVEN))
    block = (panel, part)

    def vmem(*shape):
        return pltpu.VMEM(shape, jnp.float32)

    def whole(array):
        return pl.BlockSpec(array.shape, lambda c, *_: (0, 0, 0), pipeline_mode=pl.Buffered(1))

    tops, low = pl.pallas_call(
        functools.partial(pipeline_kernel, count, turns, lag),
        out_shape=(
            jax.ShapeDtypeStruct((top_rows, columns), jnp.float32),
            jax.ShapeDtypeStruct((rows - top_rows, columns), jnp.float32),
        ),
        grid_spec=pltpu.PrefetchScalarGridSpec(
            num_scalar_prefetch=3,
            grid=(turns + lag,),
            in_specs=[
                pl.BlockSpec((rows, width), lambda c, *_: (0, jnp.minimum(c, turns - 1))),
                whole(leaf_vectors),
                whole(leaf_factors),
                whole(tree_vectors),
                whole(tree_factors),
            ],
            out_specs=[
                pl.BlockSpec((top_rows, width), lambda c, *_: (0, jnp.maximum(c - lag, 0))),
                pl.BlockSpec((rows - top_rows, width), lambda c, *_: (0, jnp.minimum(c, turns - 1))),
            ],
            scratch_shapes=[
                *[pltpu.VMEM((steps, leaf_rows, panel), short)] * 2,
                *[pltpu.VMEM((steps, panel, leaf_rows), short)] * 2,
                *[pltpu.VMEM((steps, panel, panel), short)] * 6,
                vmem(rows // BLK, BLK, width),
                vmem(turns, steps, panel, width),
                vmem(turns, steps, 2, *block),
                vmem(turns, half, *block),
                vmem(value_count, *block),
                vmem(turns, SLOTS, *block),
                vmem(turns, SLOTS, *block),
                vmem(turns, half, *block),
                vmem(turns, 2 * steps, *block),
                vmem(2, panel, panel),
                vmem(2 * panel + 8, panel),
                vmem(chips, 2 * panel + 8, panel),
                vmem(turns, 2, *block),
                *[pltpu.VMEM((chips, 2 * panel, panel), short)] * 4,
                dma((2,)),
                dma((2,)),
                dma,
                dma((chips,)),
                dma((chips,)),
                dma((chips,)),
                dma,
                dma((turns, 2 * steps)),
                dma((turns, half)),
                dma((turns, 2)),
                dma((turns, 2)),
                dma((turns,)),
                dma((turns,)),
                dma((turns, half)),
                dma((turns, 2 * steps)),
            ],
        ),
        compiler_params=pltpu.CompilerParams(
            collective_id=0, has_side_effects=True, vmem_limit_bytes=60 * 2**20
        ),
    )(
        leaf_blocks, owner, jnp.asarray(plan(count).reshape(-1)),
        matrix, leaf_vectors, leaf_factors, tree_vectors, tree_factors,
    )
    return jnp.concatenate([tops, low], axis=0)


def shards(*arrays):
    row_count = lax.axis_size("row")
    if row_count == PLANNED_ROWS:
        return pipeline(row_count, *arrays)
    return spread_shards(*arrays)


def solution(mesh):
    return jax.shard_map(
        shards,
        mesh=mesh,
        in_specs=(
            P(("groups", "row"), None),
            P("groups", "row", None),
            P("groups", "row", None),
            P("groups", "row", None),
            P("groups", "row", None),
            P("groups", "row"),
            P("groups"),
        ),
        out_specs=P(("groups", "row"), None),
        check_vma=False,
    )
```
